256 devices in a mesh: ctx: 32 (over x, y, core), head: 8 (over z).
Axes of the slice: x: 4, y: 4, z: 8, core: 2. Of those that a mesh axis runs over, the one named last changes fastest.
Arguments:
- queries: bfloat16 [2, 6144, 4096], P(None, 'ctx', 'head'), may hold values from -6 to 6
- key_rows: bfloat16 [2, 6144, 4096], P(None, 'ctx', 'head'), may hold values from -6 to 6
- value_rows: bfloat16 [2, 6144, 4096], P(None, 'ctx', 'head'), may hold values from -6 to 6
- out_weight: bfloat16 [4096, 4096], P('head'), may hold values from -0.09375 to 0.09375
- cotangent: bfloat16 [2, 6144, 4096], P(None, 'ctx', 'head'), may hold values from -6 to 6
Outputs:
- layer_output: bfloat16 [2, 6144, 4096], P(None, 'ctx', 'head')
- query_grad: bfloat16 [2, 6144, 4096], P(None, 'ctx', 'head')
- key_grad: bfloat16 [2, 6144, 4096], P(None, 'ctx', 'head')
- value_grad: bfloat16 [2, 6144, 4096], P(None, 'ctx', 'head')
- weight_grad: float32 [4096, 4096], P('head', 'ctx')
The draws below stay inside these ranges and needn't reach their ends.
All inputs are finite; a program needn't handle non-finite values.
Results may differ from the reference program's by a relative error of at most 0.015.
Values may be sent and summed in bfloat16 or wider, within the bound.
No kernel may reach another device: no remote copies, remote signals or barrier semaphores. Data moves between devices by JAX's collectives and lax.ppermute only.
A program may use at most 128 MiB of HBM per device.

```python
import jax
import jax.numpy as jnp
from jax import lax

D = 4096
HEADS = 32
DH = 128
TOK_DEV = 192
HD = 4096
TOKENS = 6144
N_CTX = 32


def spiked(values, key, source, target, parts, factor):
    owner, partner = [(jnp.arange(values.shape[dim]) // (values.shape[dim] // parts)).reshape([-1 if axis == dim else 1 for axis in range(values.ndim)]) for dim in (source, target)]
    chosen = jax.random.permutation(key, parts)[partner]
    strong = (owner == chosen) | (owner == (partner + parts // 2) % parts)
    return jnp.where(strong, factor * values, values)


def block_scale(key, shape, shards, smallest, largest):
    loudness = 1.0
    for dim, parts in shards:
        steps = jax.random.uniform(jax.random.fold_in(jax.random.fold_in(key, 6), dim), (parts,), jnp.float32, smallest / len(shards), largest / len(shards))
        loudness = loudness * jnp.repeat(jnp.exp(steps), shape[dim] // parts).reshape((-1,) + (1,) * (len(shape) - 1 - dim))
    return loudness


def bell_draw(key, shape, scale, bound, cuts=(), dtype=jnp.bfloat16):
    entries = scale * jax.random.normal(key, shape, jnp.float32)
    if cuts:
        entries = entries * block_scale(key, shape, cuts, -0.22, 0.18)
    return jnp.clip(entries, -bound, bound).astype(dtype)


def noise_with(stream_key, extent, width, most, split, heavy, held_as=jnp.bfloat16):
    values = width * jax.random.normal(stream_key, extent, jnp.float32)
    if split:
        values = values * block_scale(stream_key, extent, split, -0.22, 0.18)
    return jnp.clip(spiked(values, jax.random.fold_in(stream_key, 3), *heavy), -most, most).astype(held_as)


def setup_inputs(seed: int = 0) -> dict:
    splits = jax.random.split(jax.random.key(seed), 6)
    queries = bell_draw(splits[0], (2, TOKENS, HD), 1.0, 6.0, ((1, 32), (2, 8)))
    key_rows = bell_draw(splits[1], (2, TOKENS, HD), 1.0, 6.0, ((1, 32), (2, 8)))
    value_rows = bell_draw(splits[2], (2, TOKENS, HD), 1.0, 6.0, ((1, 32), (2, 8)))
    out_weight = bell_draw(splits[3], (HD, D), HD ** -0.5, 0.09375, ((0, 8),))
    cotangent = noise_with(splits[4], (2, TOKENS, D), 1.0, 6.0, ((1, 32), (2, 8)), (1, 2, 32, 2.75))
    return {"queries": queries, "key_rows": key_rows, "value_rows": value_rows, "out_weight": out_weight, "cotangent": cotangent}


epsilon = 1e-06

def to_blocks(array):
    return array.reshape(2, N_CTX, TOK_DEV, HEADS, DH).transpose(1, 0, 3, 2, 4)

def from_blocks(array):
    return array.transpose(1, 0, 3, 2, 4).reshape(2, N_CTX * TOK_DEV, HEADS * DH)

def rms_normalize(attended):
    return attended / jnp.sqrt(lax.optimization_barrier(jnp.mean(attended * attended, axis=-1, keepdims=True)) + epsilon)

def causal_mask():
    rows_index = lax.broadcasted_iota(jnp.int32, (TOK_DEV, TOK_DEV), 0)
    cols_index = lax.broadcasted_iota(jnp.int32, (TOK_DEV, TOK_DEV), 1)
    return rows_index >= cols_index

def reference(queries, key_rows, value_rows, out_weight, cotangent):
    head_scale = DH ** (-0.5)
    lower = causal_mask()
    query_blocks = to_blocks(queries)
    key_blocks = to_blocks(key_rows)
    value_blocks = to_blocks(value_rows)

    def block_scores(query_block, key_block):
        raw = jnp.einsum('bhtd,bhsd->bhts', query_block.astype(jnp.float32), key_block.astype(jnp.float32)) * head_scale
        return jnp.where(lower, raw, 0.0).astype(jnp.bfloat16)

    def forward_step(carry, inputs):
        query_block, key_block, value_block = inputs
        scores = block_scores(query_block, key_block)
        state_bf = carry.astype(jnp.bfloat16).astype(jnp.float32)
        attended = jnp.einsum('bhts,bhsd->bhtd', scores.astype(jnp.float32), value_block.astype(jnp.float32))
        attended = attended + head_scale * jnp.einsum('bhtd,bhde->bhte', query_block.astype(jnp.float32), state_bf)
        updated = carry + jnp.einsum('bhsd,bhse->bhde', key_block.astype(jnp.float32), value_block.astype(jnp.float32))
        return (updated, (attended, carry))
    start_state = jnp.zeros((2, HEADS, DH, DH), jnp.float32)
    final_state, (attended, states) = lax.scan(forward_step, start_state, (query_blocks, key_blocks, value_blocks))
    normed = from_blocks(rms_normalize(attended).astype(jnp.bfloat16))
    normed_flat = normed.reshape(2 * TOKENS, HD)
    layer_output = jnp.dot(normed_flat, out_weight, preferred_element_type=jnp.float32).astype(jnp.bfloat16).reshape(2, TOKENS, D)
    grad_flat = cotangent.reshape(2 * TOKENS, D)
    normed_grad = jnp.dot(grad_flat, out_weight.T, preferred_element_type=jnp.float32).reshape(2, TOKENS, HD)
    weight_grad = jnp.dot(normed_flat.T, grad_flat, preferred_element_type=jnp.float32) * (2 * TOKENS) ** (-0.5)
    pullback = jax.vjp(rms_normalize, attended)[1]
    attended_grad = pullback(to_blocks(normed_grad))[0].astype(jnp.bfloat16)

    def backward_step(carry, inputs):
        query_block, key_block, value_block, grad_block, state = inputs
        scores = block_scores(query_block, key_block).astype(jnp.float32)
        grad_f = grad_block.astype(jnp.float32)
        query_f = query_block.astype(jnp.float32)
        key_f = key_block.astype(jnp.float32)
        value_f = value_block.astype(jnp.float32)
        raw = jnp.einsum('bhtd,bhsd->bhts', grad_f, value_f) * head_scale
        score_grad = jnp.where(lower, raw, 0.0).astype(jnp.bfloat16).astype(jnp.float32)
        state_bf = state.astype(jnp.bfloat16).astype(jnp.float32)
        grad_state_bf = carry.astype(jnp.bfloat16).astype(jnp.float32)
        query_part = jnp.einsum('bhts,bhsd->bhtd', score_grad, key_f) + head_scale * jnp.einsum('bhte,bhde->bhtd', grad_f, state_bf)
        key_part = jnp.einsum('bhts,bhtd->bhsd', score_grad, query_f) + head_scale * jnp.einsum('bhse,bhde->bhsd', value_f, grad_state_bf)
        value_part = jnp.einsum('bhts,bhte->bhse', scores, grad_f) + head_scale * jnp.einsum('bhsd,bhde->bhse', key_f, grad_state_bf)
        updated = carry + jnp.einsum('bhtd,bhte->bhde', query_f, grad_f)
        return (updated, (query_part.astype(jnp.bfloat16), key_part.astype(jnp.bfloat16), value_part.astype(jnp.bfloat16)))
    last_grad, (query_grad, key_grad, value_grad) = lax.scan(backward_step, start_state, (query_blocks, key_blocks, value_blocks, attended_grad, states), reverse=True)
    return (layer_output, from_blocks(query_grad), from_blocks(key_grad), from_blocks(value_grad), weight_grad)
```

```python
import functools

import jax
import jax.numpy as jnp
from jax import lax
from jax.experimental import pallas as pl
from jax.experimental.pallas import tpu as pltpu
from jax.sharding import Mesh
from jax.sharding import PartitionSpec as P

DH = 128
CTX = ("ctx_0", "ctx_1", "ctx_2")
SCALE = DH ** (-0.5)
EPS = 1e-06
F32, BF16 = jnp.float32, jnp.bfloat16
VMEM = pltpu.VMEM


def dot(a, b, ca, cb):
    return lax.dot_general(a, b, (((ca,), (cb,)), ((), ())), preferred_element_type=F32)


def call(body, outs, args, flops, **kw):
    size = sum(a.size * a.dtype.itemsize for a in args)
    size += sum(o.size * o.dtype.itemsize for o in outs)
    cost = pl.CostEstimate(flops=flops, bytes_accessed=size, transcendentals=0)
    return pl.pallas_call(body, out_shape=outs, cost_estimate=cost, **kw)(*args)


def shape(dims, dtype):
    return jax.ShapeDtypeStruct(dims, dtype)


def lower_mask(n):
    return lax.broadcasted_iota(jnp.int32, (n, n), 0) >= lax.broadcasted_iota(jnp.int32, (n, n), 1)


def heads(width):
    return [(b, h, slice(h * DH, (h + 1) * DH)) for b in range(2) for h in range(width // DH)]


def state_body(k_ref, v_ref, out_ref):
    for i, (b, _, s) in enumerate(heads(k_ref.shape[2])):
        out_ref[i] = dot(k_ref[b, :, s], v_ref[b, :, s], 0, 0).astype(BF16)


def scan_body(reverse, x_ref, out_ref):
    total = jnp.zeros(x_ref.shape[1:], F32)
    n = x_ref.shape[0]
    for k in reversed(range(n)) if reverse else range(n):
        out_ref[k] = total.astype(BF16)
        total = total + x_ref[k].astype(F32)


def forward_body(q_ref, k_ref, v_ref, state_ref, normed_ref, attended_ref, scores_ref):
    lower = lower_mask(q_ref.shape[1])
    for i, (b, _, s) in enumerate(heads(q_ref.shape[2])):
        q, v = q_ref[b, :, s], v_ref[b, :, s]
        scores = jnp.where(lower, dot(q, k_ref[b, :, s], 1, 1) * SCALE, 0.0).astype(BF16)
        scores_ref[i] = scores
        attended = dot(scores, v, 1, 0) + SCALE * dot(q, state_ref[i], 1, 0)
        attended_ref[b, :, s] = attended
        mean = jnp.mean(attended * attended, axis=-1, keepdims=True)
        normed_ref[b, :, s] = (attended / jnp.sqrt(mean + EPS)).astype(BF16)


def project_body(n_ref, w_ref, out_ref):
    out_ref[0] = dot(n_ref[...], w_ref[...], 1, 0).astype(BF16)


def grad_body(c_ref, w_ref, a_ref, q_ref, ag_ref, gs_ref, acc_ref):
    k = pl.program_id(0)

    @pl.when(k == 0)
    def _():
        acc_ref[...] = jnp.zeros_like(acc_ref)

    acc_ref[...] += dot(c_ref[0], w_ref[...], 1, 1)

    @pl.when(k == pl.num_programs(0) - 1)
    def _():
        n = a_ref.shape[0] // 2
        for i, (b, _, s) in enumerate(heads(a_ref.shape[1])):
            rows = slice(b * n, (b + 1) * n)
            a, g = a_ref[rows, s], acc_ref[rows, s]
            root = 1.0 / jnp.sqrt(jnp.mean(a * a, axis=-1, keepdims=True) + EPS)
            inner = jnp.mean(g * a, axis=-1, keepdims=True)
            ag = (g * root - a * (inner * root * root * root)).astype(BF16)
            ag_ref[rows, s] = ag
            gs_ref[i] = dot(q_ref[rows, s], ag, 0, 0).astype(BF16)


def weight_body(place, n_ref, c_ref, out_ref, nt_ref):
    k = pl.program_id(0)

    @pl.when(k == 0)
    def _():
        nt_ref[...] = n_ref[...].T

    half = nt_ref.shape[0] // 2
    mx, my, odd = place[0], place[1], place[2] == 1
    c = c_ref[0]
    pick = jnp.concatenate(
        [jnp.where(odd, c[:, DH : 2 * DH], c[:, :DH]), jnp.where(odd, c[:, 3 * DH :], c[:, 2 * DH : 3 * DH])],
        axis=1,
    )
    r = dot(nt_ref[...], pick, 1, 0).astype(BF16)
    x = k // 2
    for j in range(2):
        y = 2 * (k % 2) + j
        piece = r[:, j * DH : (j + 1) * DH]
        out_ref[0, (y - my + 4) % 4, x] = piece[:half]
        out_ref[1, (x - mx + 4) % 4, y] = piece[half:]


def backward_body(q_ref, k_ref, v_ref, sc_ref, ag_ref, st_ref, gs_ref, dq_ref, dk_ref, dv_ref):
    lower = lower_mask(q_ref.shape[1])
    for i, (b, _, s) in enumerate(heads(q_ref.shape[2])):
        q, k, v, ag = q_ref[b, :, s], k_ref[b, :, s], v_ref[b, :, s], ag_ref[b, :, s]
        sg = jnp.where(lower, dot(ag, v, 1, 1) * SCALE, 0.0).astype(BF16)
        dq_ref[b, :, s] = (dot(sg, k, 1, 0) + SCALE * dot(ag, st_ref[i], 1, 1)).astype(BF16)
        dk_ref[b, :, s] = (dot(sg, q, 0, 0) + SCALE * dot(v, gs_ref[i], 1, 1)).astype(BF16)
        dv_ref[b, :, s] = (dot(sc_ref[i], ag, 0, 0) + SCALE * dot(k, gs_ref[i], 1, 0)).astype(BF16)


def exclusive(local, reverse):
    n = lax.axis_size(CTX)
    pieces = local.reshape(n, -1, DH)
    got = lax.all_to_all(pieces, CTX, split_axis=0, concat_axis=0, tiled=True)
    sums = call(
        functools.partial(scan_body, reverse), [shape(got.shape, BF16)], [got], got.size
    )[0]
    back = lax.all_to_all(sums, CTX, split_axis=0, concat_axis=0, tiled=True)
    return back.reshape(local.shape)


def shift(value, axis, step):
    n = lax.axis_size(axis)
    return lax.ppermute(value, axis, [(i, (i + step) % n) for i in range(n)])


def reduce_weight(term_for, factor):
    mx, my, mc = (lax.axis_index(a) for a in CTX)
    theirs = shift(term_for(jnp.stack([mx, my, 1 - mc]).astype(jnp.int32)), "ctx_2", 1)
    mine = term_for(jnp.stack([mx, my, mc]).astype(jnp.int32))
    total = (mine.astype(F32) + theirs.astype(F32)).astype(BF16)
    first = [[shift(total[i, d], axis, d) for d in (1, 2, 3)] for i, axis in ((0, "ctx_1"), (1, "ctx_0"))]
    done = []
    for i, axis, me in ((0, "ctx_0", mx), (1, "ctx_1", my)):
        part = total[i, 0].astype(F32) + sum(p.astype(F32) for p in first[i])
        send = part.astype(BF16)
        got = [
            shift(lax.dynamic_index_in_dim(send, (me + d) % 4, 0, False), axis, d) for d in (1, 2, 3)
        ]
        own = lax.dynamic_index_in_dim(part, me, 0, False)
        done.append(own + sum(g.astype(F32) for g in got))
    return jnp.concatenate(done, axis=0) * factor


def shards(queries, key_rows, value_rows, out_weight, cotangent):
    _, length, width = queries.shape
    n_head = lax.axis_size("head")
    rows = 2 * length
    n_mat = 2 * width // DH
    square = (n_mat, DH, DH)
    gathered = lax.all_gather(cotangent, "head", axis=0, tiled=False).reshape(n_head, rows, width)
    mat_flops = 2 * n_mat * length * DH * DH
    local = call(state_body, [shape(square, BF16)], [key_rows, value_rows], mat_flops)[0]
    state = exclusive(local, False)
    normed, attended, scores = call(
        forward_body,
        [shape(queries.shape, BF16), shape(queries.shape, F32), shape((n_mat, length, length), BF16)],
        [queries, key_rows, value_rows, state],
        5 * mat_flops,
    )
    normed = normed.reshape(rows, width)
    big = 2 * rows * width * width * n_head
    partial = call(
        project_body,
        [shape((n_head, rows, width), BF16)],
        [normed, out_weight],
        big,
        grid=(n_head,),
        in_specs=[
            pl.BlockSpec((rows, width), lambda k: (0, 0)),
            pl.BlockSpec((width, width), lambda k: (0, k)),
        ],
        out_specs=[pl.BlockSpec((1, rows, width), lambda k: (k, 0, 0))],
    )[0]
    layer_output = lax.psum_scatter(
        partial.reshape(n_head * rows, width), "head", scatter_dimension=0, tiled=True
    ).reshape(queries.shape)
    attended_grad, local_grad = call(
        grad_body,
        [shape((rows, width), BF16), shape(square, BF16)],
        [gathered, out_weight, attended.reshape(rows, width), queries.reshape(rows, width)],
        big,
        grid=(n_head,),
        in_specs=[
            pl.BlockSpec((1, rows, width), lambda k: (k, 0, 0)),
            pl.BlockSpec((width, width), lambda k: (0, k)),
            pl.BlockSpec((rows, width), lambda k: (0, 0)),
            pl.BlockSpec((rows, width), lambda k: (0, 0)),
        ],
        out_specs=[
            pl.BlockSpec((rows, width), lambda k: (0, 0)),
            pl.BlockSpec(square, lambda k: (0, 0, 0)),
        ],
        scratch_shapes=[VMEM((rows, width), F32)],
    )

    def weight_term(place):
        return call(
            weight_body,
            [shape((2, 4, 4, width // 2, DH), BF16)],
            [place, normed, gathered],
            big // 2,
            grid_spec=pltpu.PrefetchScalarGridSpec(
                num_scalar_prefetch=1,
                grid=(n_head,),
                in_specs=[
                    pl.BlockSpec((rows, width), lambda k, _: (0, 0)),
                    pl.BlockSpec((1, rows, width), lambda k, _: (k, 0, 0)),
                ],
                out_specs=[pl.BlockSpec((2, 4, 4, width // 2, DH), lambda k, _: (0, 0, 0, 0, 0))],
                scratch_shapes=[VMEM((width, rows), BF16)],
            ),
        )[0]

    weight_grad = reduce_weight(weight_term, (rows * lax.axis_size(CTX)) ** (-0.5))
    grad_state = exclusive(local_grad, True)
    query_grad, key_grad, value_grad = call(
        backward_body,
        [shape(queries.shape, BF16)] * 3,
        [queries, key_rows, value_rows, scores, attended_grad.reshape(queries.shape), state, grad_state],
        10 * mat_flops,
    )
    return (layer_output, query_grad, key_grad, value_grad, weight_grad)


def solution(mesh):
    split = Mesh(
        mesh.devices.reshape(4, 4, 2, mesh.shape["head"]), ("ctx_0", "ctx_1", "ctx_2", "head")
    )
    rows = P(None, CTX, "head")
    return jax.shard_map(
        shards,
        mesh=split,
        in_specs=(rows, rows, rows, P("head", None), rows),
        out_specs=(rows, rows, rows, rows, P("head", CTX)),
        check_vma=False,
    )
```

```python
import functools

import jax
import jax.numpy as jnp
from jax import lax
from jax.experimental import pallas as pl
from jax.experimental.pallas import tpu as pltpu
from jax.sharding import Mesh
from jax.sharding import PartitionSpec as P

DH = 128
CTX = ("ctx_0", "ctx_1", "ctx_2")
SCALE = DH ** (-0.5)
EPS = 1e-06
F32, BF16 = jnp.float32, jnp.bfloat16
VMEM = pltpu.VMEM
LIMIT, FULL = 24 << 20, 123 << 19


def dot(a, b, ca, cb):
    return lax.dot_general(a, b, (((ca,), (cb,)), ((), ())), preferred_element_type=F32)


def call(body, outs, args, flops, limit=LIMIT, **kw):
    size = sum(a.size * a.dtype.itemsize for a in args)
    size += sum(o.size * o.dtype.itemsize for o in outs)
    cost = pl.CostEstimate(flops=flops, bytes_accessed=size, transcendentals=0)
    params = pltpu.CompilerParams(vmem_limit_bytes=limit)
    return pl.pallas_call(body, out_shape=outs, cost_estimate=cost, compiler_params=params, **kw)(*args)


def shape(dims, dtype):
    return jax.ShapeDtypeStruct(dims, dtype)


def lower_mask(n):
    return lax.broadcasted_iota(jnp.int32, (n, n), 0) >= lax.broadcasted_iota(jnp.int32, (n, n), 1)


def heads(width):
    return [(b, h, slice(h * DH, (h + 1) * DH)) for b in range(2) for h in range(width // DH)]


def state_body(k_ref, v_ref, out_ref):
    for i, (b, _, s) in enumerate(heads(k_ref.shape[2])):
        out_ref[i] = dot(k_ref[b, :, s], v_ref[b, :, s], 0, 0).astype(BF16)


def scan_body(reverse, x_ref, out_ref):
    total = jnp.zeros(x_ref.shape[1:], F32)
    n = x_ref.shape[0]
    for k in reversed(range(n)) if reverse else range(n):
        out_ref[k] = total.astype(BF16)
        total = total + x_ref[k].astype(F32)


def forward_body(q_ref, k_ref, v_ref, state_ref, normed_ref, attended_ref, scores_ref):
    lower = lower_mask(q_ref.shape[1])
    for i, (b, _, s) in enumerate(heads(q_ref.shape[2])):
        q, v = q_ref[b, :, s], v_ref[b, :, s]
        scores = jnp.where(lower, dot(q, k_ref[b, :, s], 1, 1) * SCALE, 0.0).astype(BF16)
        scores_ref[i] = scores
        attended = dot(scores, v, 1, 0) + SCALE * dot(q, state_ref[i], 1, 0)
        attended_ref[b, :, s] = attended
        mean = jnp.mean(attended * attended, axis=-1, keepdims=True)
        normed_ref[b, :, s] = (attended / jnp.sqrt(mean + EPS)).astype(BF16)


def project_body(n_ref, w_hbm, out_hbm, w_buf, out_buf, w_sem, out_sem):
    chunks, _, width = w_buf.shape
    copies = []
    for k in range(chunks):
        copies.append(
            pltpu.make_async_copy(w_hbm.at[:, k * width : (k + 1) * width], w_buf.at[k], w_sem.at[k])
        )
        copies[k].start()
    done = []
    for k in range(chunks):
        copies[k].wait()
        out_buf[k] = dot(n_ref[...], w_buf[k], 1, 0).astype(BF16)
        done.append(pltpu.make_async_copy(out_buf.at[k], out_hbm.at[k], out_sem.at[k]))
        done[k].start()
    for copy in done:
        copy.wait()


def grad_body(c_hbm, w_hbm, a_ref, q_ref, ag_ref, gs_ref, c_buf, w_buf, c_sem, w_sem):
    chunks, rows, width = c_buf.shape
    copies = []
    for k in range(chunks):
        cols = slice(k * width, (k + 1) * width)
        pair = (
            pltpu.make_async_copy(c_hbm.at[k], c_buf.at[k], c_sem.at[k]),
            pltpu.make_async_copy(w_hbm.at[:, cols], w_buf.at[k], w_sem.at[k]),
        )
        for copy in pair:
            copy.start()
        copies.append(pair)
    total = jnp.zeros((rows, width), F32)
    for k in range(chunks):
        for copy in copies[k]:
            copy.wait()
        total = total + dot(c_buf[k], w_buf[k], 1, 1)
    n = rows // 2
    for i, (b, _, s) in enumerate(heads(width)):
        part = slice(b * n, (b + 1) * n)
        a, g = a_ref[part, s], total[part, s]
        root = 1.0 / jnp.sqrt(jnp.mean(a * a, axis=-1, keepdims=True) + EPS)
        inner = jnp.mean(g * a, axis=-1, keepdims=True)
        ag = (g * root - a * (inner * root * root * root)).astype(BF16)
        ag_ref[part, s] = ag
        gs_ref[i] = dot(q_ref[part, s], ag, 0, 0).astype(BF16)


def weight_pieces(place, n_ref, c_hbm, c_buf, c_sem):
    chunks = c_buf.shape[0]
    copies = [pltpu.make_async_copy(c_hbm.at[k], c_buf.at[k], c_sem.at[k]) for k in range(chunks)]
    for copy in copies:
        copy.start()
    left = n_ref[...].T
    mx, my, mc = place[0], place[1], place[2]
    low = pl.multiple_of(mc * DH, DH)
    high = pl.multiple_of(mc * DH + 2 * DH, DH)
    for k in range(chunks):
        copies[k].wait()
        pick = jnp.concatenate([c_buf[k, :, pl.ds(low, DH)], c_buf[k, :, pl.ds(high, DH)]], axis=1)
        r = dot(left, pick, 1, 0)
        x = k // 2
        for j in range(2):
            y = 2 * (k % 2) + j
            far = jnp.where(mc == 0, (y - my + 4) % 4, (x - mx + 4) % 4)
            yield far, jnp.where(mc == 0, x, y), r[:, j * DH : (j + 1) * DH]


def weight_body(place, n_ref, c_hbm, out_ref, c_buf, c_sem):
    for far, other, piece in weight_pieces(place, n_ref, c_hbm, c_buf, c_sem):
        out_ref[far, other] = piece.astype(BF16)


def weight_add_body(place, n_ref, c_hbm, in_ref, o0, o1, o2, o3, c_buf, c_sem):
    def put(far, other, value):
        for d, ref in enumerate((o0, o1, o2, o3)):

            @pl.when(far == d)
            def _():
                ref[other] = value

    for far, other, piece in weight_pieces(place, n_ref, c_hbm, c_buf, c_sem):
        put(far, other, (piece + in_ref[far, other].astype(F32)).astype(BF16))


def backward_body(q_ref, k_ref, v_ref, sc_ref, ag_ref, st_ref, gs_ref, dq_ref, dk_ref, dv_ref):
    lower = lower_mask(q_ref.shape[1])
    for i, (b, _, s) in enumerate(heads(q_ref.shape[2])):
        q, k, v, ag = q_ref[b, :, s], k_ref[b, :, s], v_ref[b, :, s], ag_ref[b, :, s]
        sg = jnp.where(lower, dot(ag, v, 1, 1) * SCALE, 0.0).astype(BF16)
        dq_ref[b, :, s] = (dot(sg, k, 1, 0) + SCALE * dot(ag, st_ref[i], 1, 1)).astype(BF16)
        dk_ref[b, :, s] = (dot(sg, q, 0, 0) + SCALE * dot(v, gs_ref[i], 1, 1)).astype(BF16)
        dv_ref[b, :, s] = (dot(sc_ref[i], ag, 0, 0) + SCALE * dot(k, gs_ref[i], 1, 0)).astype(BF16)


def exclusive(local, reverse):
    n = lax.axis_size(CTX)
    pieces = local.reshape(n, -1, DH)
    got = lax.all_to_all(pieces, CTX, split_axis=0, concat_axis=0, tiled=True)
    sums = call(
        functools.partial(scan_body, reverse), [shape(got.shape, BF16)], [got], got.size
    )[0]
    back = lax.all_to_all(sums, CTX, split_axis=0, concat_axis=0, tiled=True)
    return back.reshape(local.shape)


def shift(value, axis, step):
    n = lax.axis_size(axis)
    return lax.ppermute(value, axis, [(i, (i + step) % n) for i in range(n)])


def shift_by_core(value, first, step):
    def target(x, y, c):
        along_y = (c == 0) == first
        return (x, (y + step) % 4, c) if along_y else ((x + step) % 4, y, c)

    def index(x, y, c):
        return (x * 4 + y) * 2 + c

    places = [(x, y, c) for x in range(4) for y in range(4) for c in range(2)]
    return lax.ppermute(value, CTX, [(index(*p), index(*target(*p))) for p in places])


def reduce_weight(normed, gathered, factor, after):
    mx, my, mc = (lax.axis_index(a) for a in CTX)
    chunks, rows, width = gathered.shape
    flops = rows * width * width * chunks
    grid = (4, 4, width, DH)
    scratch = [VMEM(gathered.shape, BF16), pltpu.SemaphoreType.DMA((chunks,))]
    smem, vmem, hbm = (pl.BlockSpec(memory_space=m) for m in (pltpu.SMEM, VMEM, pltpu.HBM))
    theirs = call(
        weight_body,
        [shape(grid, BF16)],
        [jnp.stack([mx, my, 1 - mc]).astype(jnp.int32), normed, gathered],
        flops,
        limit=FULL,
        in_specs=[smem, vmem, hbm],
        out_specs=[vmem],
        scratch_shapes=scratch,
    )[0]
    theirs, _ = lax.optimization_barrier((shift(theirs, "ctx_2", 1), after))
    total = call(
        weight_add_body,
        [shape(grid[1:], BF16)] * 4,
        [jnp.stack([mx, my, mc]).astype(jnp.int32), normed, gathered, theirs],
        flops,
        limit=FULL,
        in_specs=[smem, vmem, hbm, vmem],
        out_specs=[vmem] * 4,
        scratch_shapes=scratch,
    )
    got = [shift_by_core(total[d], True, d) for d in (1, 2, 3)]
    part = total[0].astype(F32) + sum(g.astype(F32) for g in got)
    send = part.astype(BF16)
    me = jnp.where(mc == 0, mx, my)
    got = [
        shift_by_core(lax.dynamic_index_in_dim(send, (me + d) % 4, 0, False), False, d)
        for d in (1, 2, 3)
    ]
    own = lax.dynamic_index_in_dim(part, me, 0, False)
    return (own + sum(g.astype(F32) for g in got)) * factor


def layer(queries, key_rows, value_rows, out_weight, cotangent):
    _, length, width = queries.shape
    n_head = lax.axis_size("head")
    rows = 2 * length
    n_mat = 2 * width // DH
    square = (n_mat, DH, DH)
    gathered = lax.all_gather(cotangent, "head", axis=0, tiled=False).reshape(n_head, rows, width)
    mat_flops = 2 * n_mat * length * DH * DH
    local = call(state_body, [shape(square, BF16)], [key_rows, value_rows], mat_flops)[0]
    state = exclusive(local, False)
    normed, attended, scores = call(
        forward_body,
        [shape(queries.shape, BF16), shape(queries.shape, F32), shape((n_mat, length, length), BF16)],
        [queries, key_rows, value_rows, state],
        5 * mat_flops,
    )
    normed = normed.reshape(rows, width)
    big = 2 * rows * width * width * n_head
    partial = call(
        project_body,
        [shape((n_head, rows, width), BF16)],
        [normed, out_weight],
        big,
        limit=FULL,
        in_specs=[pl.BlockSpec(memory_space=VMEM), pl.BlockSpec(memory_space=pltpu.HBM)],
        out_specs=[pl.BlockSpec(memory_space=pltpu.HBM)],
        scratch_shapes=[
            VMEM((n_head, width, width), BF16),
            VMEM((n_head, rows, width), BF16),
            pltpu.SemaphoreType.DMA((n_head,)),
            pltpu.SemaphoreType.DMA((n_head,)),
        ],
    )[0]
    layer_output = lax.psum_scatter(
        partial.reshape(n_head * rows, width), "head", scatter_dimension=0, tiled=True
    ).reshape(queries.shape)
    attended_grad, local_grad = call(
        grad_body,
        [shape((rows, width), BF16), shape(square, BF16)],
        [gathered, out_weight, attended.reshape(rows, width), queries.reshape(rows, width)],
        big,
        limit=FULL,
        in_specs=[pl.BlockSpec(memory_space=m) for m in (pltpu.HBM, pltpu.HBM, VMEM, VMEM)],
        scratch_shapes=[
            VMEM(gathered.shape, BF16),
            VMEM((n_head, width, width), BF16),
            pltpu.SemaphoreType.DMA((n_head,)),
            pltpu.SemaphoreType.DMA((n_head,)),
        ],
    )
    weight_grad = reduce_weight(
        normed, gathered, (rows * lax.axis_size(CTX)) ** (-0.5), local_grad
    )
    grad_state = exclusive(local_grad, True)
    query_grad, key_grad, value_grad = call(
        backward_body,
        [shape(queries.shape, BF16)] * 3,
        [queries, key_rows, value_rows, scores, attended_grad.reshape(queries.shape), state, grad_state],
        10 * mat_flops,
    )
    return (layer_output, query_grad, key_grad, value_grad, weight_grad)


def solution(mesh):
    split = Mesh(
        mesh.devices.reshape(4, 4, 2, mesh.shape["head"]), ("ctx_0", "ctx_1", "ctx_2", "head")
    )
    rows = P(None, CTX, "head")
    return jax.shard_map(
        layer,
        mesh=split,
        in_specs=(rows, rows, rows, P("head", None), rows),
        out_specs=(rows, rows, rows, rows, P("head", CTX)),
        check_vma=False,
    )
```

```python
import functools

import jax
import jax.numpy as jnp
from jax import lax
from jax.experimental import pallas as pl
from jax.experimental.pallas import tpu as pltpu
from jax.sharding import Mesh
from jax.sharding import PartitionSpec as P

DH = 128
CTX = ("ctx_0", "ctx_1", "ctx_2")
SCALE = DH ** (-0.5)
EPS = 1e-06
F32, BF16 = jnp.float32, jnp.bfloat16
VMEM = pltpu.VMEM
LIMIT = 20 << 20
SMEM = pltpu.SMEM
STEPS = (0, -1, 1, -2, 2, -3, 3)


def dot(a, b, ca, cb):
    return lax.dot_general(a, b, (((ca,), (cb,)), ((), ())), preferred_element_type=F32)


def call(body, outs, args, flops, scalar=False, scratch=()):
    size = sum(a.size * a.dtype.itemsize for a in args)
    size += sum(o.size * o.dtype.itemsize for o in outs)
    cost = pl.CostEstimate(flops=flops, bytes_accessed=size, transcendentals=0)
    specs = [pl.BlockSpec(memory_space=VMEM)] * len(args)
    if scalar:
        specs[0] = pl.BlockSpec(memory_space=SMEM)
    return pl.pallas_call(
        body,
        out_shape=outs,
        in_specs=specs,
        out_specs=[pl.BlockSpec(memory_space=VMEM)] * len(outs),
        scratch_shapes=list(scratch),
        cost_estimate=cost,
        compiler_params=pltpu.CompilerParams(vmem_limit_bytes=LIMIT),
    )(*args)


def shape(dims, dtype):
    return jax.ShapeDtypeStruct(dims, dtype)


def lower_mask(n):
    return lax.broadcasted_iota(jnp.int32, (n, n), 0) >= lax.broadcasted_iota(jnp.int32, (n, n), 1)


def heads(width):
    return [(b, h, slice(h * DH, (h + 1) * DH)) for b in range(2) for h in range(width // DH)]


def local_states(place, left, right, keep_ref, send_ref):
    mc = place[2]
    for h in range(keep_ref.shape[0]):
        s = slice(h * DH, (h + 1) * DH)
        keep_ref[h] = dot(left[mc, :, s], right[mc, :, s], 0, 0)
        send_ref[h] = dot(left[1 - mc, :, s], right[1 - mc, :, s], 0, 0).astype(BF16)


def state_body(place, k_ref, v_ref, keep_ref, send_ref):
    local_states(place, k_ref, v_ref, keep_ref, send_ref)


def chip_body(keep_ref, got_ref, out_ref):
    out_ref[...] = (keep_ref[...] + got_ref[...].astype(F32)).astype(BF16)


def first_axis_body(reverse, place, t_ref, g1, g2, g3, own_ref, m1, m2, m3):
    rows_first = place[2] == 0
    first = jnp.where(rows_first, place[1], place[0])
    second = jnp.where(rows_first, place[0], place[1])
    chip = t_ref[...].astype(F32)
    every, some = chip, jnp.zeros_like(chip)
    for d, g in ((1, g1), (2, g2), (3, g3)):
        value = g[...].astype(F32)
        every = every + value
        taken = first < d if reverse else first >= d
        some = some + jnp.where(taken, value, 0.0)
    own_ref[...] = some
    base = jnp.where(rows_first, 0.0, some)
    extra = jnp.where(rows_first, every, chip)
    for d, m in ((1, m1), (2, m2), (3, m3)):
        given = second + d >= 4 if reverse else second + d < 4
        m[...] = (base + jnp.where(given, extra, 0.0)).astype(BF16)


def second_axis_body(reverse, place, own_ref, g1, g2, g3, keep_ref, got_ref, out_ref, send_ref):
    total = own_ref[...]
    for g in (g1, g2, g3):
        total = total + g[...].astype(F32)
    late = place[2] == (0 if reverse else 1)
    out_ref[...] = (total + jnp.where(late, got_ref[...].astype(F32), 0.0)).astype(BF16)
    send_ref[...] = (total + jnp.where(late, 0.0, keep_ref[...])).astype(BF16)


def pick_state(place, own_ref, other_ref, b, s):
    h = s.start // DH
    return jnp.where(place[2] == b, own_ref[h], other_ref[h])


def each_batch(width, step):
    def body(b, carry):
        for h in range(width // DH):
            step(b, b * (width // DH) + h, slice(h * DH, (h + 1) * DH))
        return carry

    lax.fori_loop(0, 2, body, 0)


def forward_body(place, q_ref, k_ref, v_ref, so_ref, sr_ref, normed_ref, attended_ref, scores_ref):
    lower = lower_mask(q_ref.shape[1])

    def step(b, i, s):
        q, v = q_ref[b, :, s], v_ref[b, :, s]
        scores = jnp.where(lower, dot(q, k_ref[b, :, s], 1, 1) * SCALE, 0.0).astype(BF16)
        scores_ref[i] = scores
        state = pick_state(place, so_ref, sr_ref, b, s)
        attended = dot(scores, v, 1, 0) + SCALE * dot(q, state, 1, 0)
        attended_ref[b, :, s] = attended
        mean = jnp.mean(attended * attended, axis=-1, keepdims=True)
        normed_ref[b, :, s] = (attended / jnp.sqrt(mean + EPS)).astype(BF16)

    each_batch(q_ref.shape[2], step)


def project_body(n_ref, w_ref, out_ref):
    width = n_ref.shape[1]
    for j in range(out_ref.shape[0]):
        out_ref[j] = dot(n_ref[...], w_ref[:, j * width : (j + 1) * width], 1, 0).astype(BF16)


def half_body(first, x_ref, out_ref):
    out_ref[...] = x_ref[:, first : first + out_ref.shape[1]]


def combine_body(place, o_ref, g1, g2, g3, own_ref, s1, s2, s3):
    me = jnp.where(place[2] == 0, place[0], place[1])
    for d, out in enumerate((own_ref, s1, s2, s3)):
        i = (me + d) % 4
        total = o_ref[i].astype(F32)
        for g in (g1, g2, g3):
            total = total + g[i].astype(F32)
        out[...] = total.astype(out.dtype)


def finish_body(factor, own_ref, g1, g2, g3, out_ref):
    total = own_ref[...]
    for g in (g1, g2, g3):
        total = total + g[...].astype(F32)
    out_ref[...] = total * factor


def owner_of(place, step):
    return (place[3] + step + 8) % 8


def block_dot(place, step, ref, w_ref, first=0):
    width = w_ref.shape[0]
    start = pl.multiple_of(owner_of(place, step) * width + first, DH)
    return dot(ref[...], w_ref[:, pl.ds(start, ref.shape[1])], 1, 1)


def grad_near_body(steps, place, *refs):
    *blocks, w_ref, out_ref = refs
    total = block_dot(place, steps[0], blocks[0], w_ref)
    for step, ref in zip(steps[1:], blocks[1:]):
        total = total + block_dot(place, step, ref, w_ref)
    out_ref[...] = total


def grad_far_body(steps, place, *refs):
    *blocks, r4, l4, w_ref, sum_ref, a_ref, q_ref, ag_ref, keep_ref, send_ref = refs
    rows, width = sum_ref.shape
    total = sum_ref[...]
    for step, ref in zip(steps, blocks):
        total = total + block_dot(place, step, ref, w_ref)
    total = total + block_dot(place, 4, r4, w_ref) + block_dot(place, 4, l4, w_ref, width // 2)
    n = rows // 2
    for b, _, s in heads(width):
        part = slice(b * n, (b + 1) * n)
        a, g = a_ref[b, :, s], total[part, s]
        root = 1.0 / jnp.sqrt(jnp.mean(a * a, axis=-1, keepdims=True) + EPS)
        inner = jnp.mean(g * a, axis=-1, keepdims=True)
        ag_ref[b, :, s] = (g * root - a * (inner * root * root * root)).astype(BF16)
    local_states(place, q_ref, ag_ref, keep_ref, send_ref)


def weight_pieces(steps, place, mc, n_ref, blocks):
    mx, my = place[0], place[1]
    *whole, r4, l4 = blocks
    low = pl.multiple_of(mc * DH, DH)
    high = pl.multiple_of(mc * DH + 2 * DH, DH)
    picks = [(s, ref[:, pl.ds(low, DH)], ref[:, pl.ds(high, DH)]) for s, ref in zip(steps, whole)]
    picks.append((4, r4[:, pl.ds(low, DH)], l4[:, pl.ds(low, DH)]))
    for step, left, right in picks:
        k = owner_of(place, step)
        r = dot(n_ref[...], jnp.concatenate([left, right], axis=1), 0, 0)
        x = k // 2
        for j in range(2):
            y = 2 * (k % 2) + j
            far = jnp.where(mc == 0, (y - my + 4) % 4, (x - mx + 4) % 4)
            yield far, jnp.where(mc == 0, x, y), r[:, j * DH : (j + 1) * DH]


def weight_body(steps, place, n_ref, *refs):
    *blocks, out_ref = refs
    for far, other, piece in weight_pieces(steps, place, 1 - place[2], n_ref, blocks):
        out_ref[far, other] = piece.astype(BF16)


def weight_add_body(steps, place, n_ref, *refs):
    *blocks, in_ref, o0, o1, o2, o3, buf, sem = refs
    for far, other, piece in weight_pieces(steps, place, place[2], n_ref, blocks):
        buf[far, other] = (piece + in_ref[far, other].astype(F32)).astype(BF16)
    copies = [
        pltpu.make_async_copy(buf.at[d], o, sem.at[d]) for d, o in enumerate((o0, o1, o2, o3))
    ]
    for copy in copies:
        copy.start()
    for copy in copies:
        copy.wait()


def backward_body(place, q_ref, k_ref, v_ref, sc_ref, ag_ref, so, sr, go, gr, dq_ref, dk_ref, dv_ref):
    lower = lower_mask(q_ref.shape[1])

    def step(b, i, s):
        q, k, v, ag = q_ref[b, :, s], k_ref[b, :, s], v_ref[b, :, s], ag_ref[b, :, s]
        sg = jnp.where(lower, dot(ag, v, 1, 1) * SCALE, 0.0).astype(BF16)
        earlier, later = pick_state(place, so, sr, b, s), pick_state(place, go, gr, b, s)
        dq_ref[b, :, s] = (dot(sg, k, 1, 0) + SCALE * dot(ag, earlier, 1, 1)).astype(BF16)
        dk_ref[b, :, s] = (dot(sg, q, 0, 0) + SCALE * dot(v, later, 1, 1)).astype(BF16)
        dv_ref[b, :, s] = (dot(sc_ref[i], ag, 0, 0) + SCALE * dot(k, later, 1, 0)).astype(BF16)

    each_batch(q_ref.shape[2], step)


def shift(value, axis, step):
    n = lax.axis_size(axis)
    return lax.ppermute(value, axis, [(i, (i + step) % n) for i in range(n)])


def shift_by_core(value, first, step):
    def target(x, y, c):
        along_y = (c == 0) == first
        return (x, (y + step) % 4, c) if along_y else ((x + step) % 4, y, c)

    def index(x, y, c):
        return (x * 4 + y) * 2 + c

    places = [(x, y, c) for x in range(4) for y in range(4) for c in range(2)]
    return lax.ppermute(value, CTX, [(index(*p), index(*target(*p))) for p in places])


def exclusive(place, keep, send, reverse):
    half, size = keep.shape, keep.size
    got = shift(send, "ctx_2", 1)
    chip = call(chip_body, [shape(half, BF16)], [keep, got], size)[0]
    near = []
    for d in (1, 2, 3):
        near.append(shift_by_core(chip, True, d))
    own, *out = call(
        functools.partial(first_axis_body, reverse),
        [shape(half, F32)] + [shape(half, BF16)] * 3,
        [place, chip, *near],
        size * 10,
        True,
    )
    far = []
    for d in (1, 2, 3):
        far.append(shift_by_core(out[d - 1], False, d))
    mine, other = call(
        functools.partial(second_axis_body, reverse),
        [shape(half, BF16)] * 2,
        [place, own, *far, keep, got],
        size * 8,
        True,
    )
    return mine, shift(other, "ctx_2", 1)


def gather_ring(block):
    near, right, left = [block], block, block
    rows, width = block.shape
    for i in (1, 2, 3, 4):
        if i == 4:
            half = [shape((rows, width // 2), BF16)]
            right = call(functools.partial(half_body, 0), half, [right], 0)[0]
            left = call(functools.partial(half_body, width // 2), half, [left], 0)[0]
        right = shift(right, "head", 1)
        left = shift(left, "head", -1)
        near += [right, left]
    return near


def reduce_weight(place, normed, blocks, factor, after):
    rows, width = normed.shape
    flops = rows * width * width * 8
    grid = (4, 4, width, DH)
    theirs = call(
        functools.partial(weight_body, STEPS),
        [shape(grid, BF16)],
        [place, normed, *blocks],
        flops,
        True,
    )[0]
    theirs = shift(theirs, "ctx_2", 1)
    theirs, _ = lax.optimization_barrier((theirs, after))
    total = call(
        functools.partial(weight_add_body, STEPS),
        [shape(grid[1:], BF16)] * 4,
        [place, normed, *blocks, theirs],
        flops,
        True,
        [VMEM(grid, BF16), pltpu.SemaphoreType.DMA((4,))],
    )
    got = [shift_by_core(total[d], True, d) for d in (1, 2, 3)]
    piece = (width, DH)
    own, *send = call(
        combine_body,
        [shape(piece, F32)] + [shape(piece, BF16)] * 3,
        [place, total[0], *got],
        total[0].size * 4,
        True,
    )
    got = [shift_by_core(send[d - 1], False, d) for d in (1, 2, 3)]
    return call(functools.partial(finish_body, factor), [shape(piece, F32)], [own, *got], own.size * 4)[0]


def layer(queries, key_rows, value_rows, out_weight, cotangent):
    _, length, width = queries.shape
    n_head = lax.axis_size("head")
    rows = 2 * length
    n_mat = 2 * width // DH
    half = (n_mat // 2, DH, DH)
    blocks = gather_ring(cotangent.reshape(rows, width))
    mx, my, mc, mz = (lax.axis_index(a) for a in (*CTX, "head"))
    place = jnp.stack([mx, my, mc, mz]).astype(jnp.int32)
    mat_flops = 2 * n_mat * length * DH * DH
    pair = [shape(half, F32), shape(half, BF16)]
    keep, send = call(state_body, pair, [place, key_rows, value_rows], mat_flops, True)
    state = exclusive(place, keep, send, False)
    normed, attended, scores = call(
        forward_body,
        [shape(queries.shape, BF16), shape(queries.shape, F32), shape((n_mat, length, length), BF16)],
        [place, queries, key_rows, value_rows, *state],
        5 * mat_flops,
        True,
    )
    normed = normed.reshape(rows, width)
    big = 2 * rows * width * width * n_head
    partial = call(project_body, [shape((n_head, rows, width), BF16)], [normed, out_weight], big)[0]
    layer_output = lax.psum_scatter(
        partial.reshape(n_head * rows, width), "head", scatter_dimension=0, tiled=True
    ).reshape(queries.shape)
    part_grad = call(
        functools.partial(grad_near_body, STEPS[:5]),
        [shape((rows, width), F32)],
        [place, *blocks[:5], out_weight],
        big * 5 // 8,
        True,
    )[0]
    attended_grad, keep, send = call(
        functools.partial(grad_far_body, STEPS[5:]),
        [shape(queries.shape, BF16), *pair],
        [place, *blocks[5:], out_weight, part_grad, attended, queries],
        big * 3 // 8,
        True,
    )
    factor = (rows * lax.axis_size(CTX)) ** (-0.5)
    weight_grad = reduce_weight(place, normed, blocks, factor, keep)
    grad_state = exclusive(place, keep, send, True)
    query_grad, key_grad, value_grad = call(
        backward_body,
        [shape(queries.shape, BF16)] * 3,
        [place, queries, key_rows, value_rows, scores, attended_grad, *state, *grad_state],
        10 * mat_flops,
        True,
    )
    return (layer_output, query_grad, key_grad, value_grad, weight_grad)


def solution(mesh):
    split = Mesh(
        mesh.devices.reshape(4, 4, 2, mesh.shape["head"]), ("ctx_0", "ctx_1", "ctx_2", "head")
    )
    rows = P(None, CTX, "head")
    return jax.shard_map(
        layer,
        mesh=split,
        in_specs=(rows, rows, rows, P("head", None), rows),
        out_specs=(rows, rows, rows, rows, P("head", CTX)),
        check_vma=False,
    )
```

```python
import functools

import jax
import jax.numpy as jnp
from jax import lax
from jax.experimental import pallas as pl
from jax.experimental.pallas import tpu as pltpu
from jax.sharding import Mesh
from jax.sharding import PartitionSpec as P

DH = 128
CTX = ("ctx_0", "ctx_1", "ctx_2")
SCALE = DH ** (-0.5)
EPS = 1e-06
F32, BF16 = jnp.float32, jnp.bfloat16
VMEM = pltpu.VMEM
LIMIT = 20 << 20
SMEM = pltpu.SMEM
STEPS = (0, -1, 1, -2, 2, -3, 3)


def dot(a, b, ca, cb):
    return lax.dot_general(a, b, (((ca,), (cb,)), ((), ())), preferred_element_type=F32)


def call(body, outs, args, flops, scalar=False, scratch=()):
    size = sum(a.size * a.dtype.itemsize for a in args)
    size += sum(o.size * o.dtype.itemsize for o in outs)
    cost = pl.CostEstimate(flops=flops, bytes_accessed=size, transcendentals=0)
    specs = [pl.BlockSpec(memory_space=VMEM)] * len(args)
    if scalar:
        specs[0] = pl.BlockSpec(memory_space=SMEM)
    return pl.pallas_call(
        body,
        out_shape=outs,
        in_specs=specs,
        out_specs=[pl.BlockSpec(memory_space=VMEM)] * len(outs),
        scratch_shapes=list(scratch),
        cost_estimate=cost,
        compiler_params=pltpu.CompilerParams(vmem_limit_bytes=LIMIT),
    )(*args)


def shape(dims, dtype):
    return jax.ShapeDtypeStruct(dims, dtype)


def lower_mask(n):
    return lax.broadcasted_iota(jnp.int32, (n, n), 0) >= lax.broadcasted_iota(jnp.int32, (n, n), 1)


def local_states(place, left, right, keep_ref, send_ref):
    mc = place[2]
    for h in range(keep_ref.shape[0]):
        s = slice(h * DH, (h + 1) * DH)
        keep_ref[h] = dot(left[mc, :, s], right[mc, :, s], 0, 0)
        send_ref[h] = dot(left[1 - mc, :, s], right[1 - mc, :, s], 0, 0).astype(BF16)


def state_body(place, k_ref, v_ref, keep_ref, send_ref, k_out, v_out):
    local_states(place, k_ref, v_ref, keep_ref, send_ref)
    k_out[...] = k_ref[...]
    v_out[...] = v_ref[...]


def chip_body(keep_ref, got_ref, out_ref):
    out_ref[...] = (keep_ref[...] + got_ref[...].astype(F32)).astype(BF16)


def first_axis_body(reverse, place, t_ref, g1, g2, g3, own_ref, m1, m2, m3):
    rows_first = place[2] == 0
    first = jnp.where(rows_first, place[1], place[0])
    second = jnp.where(rows_first, place[0], place[1])
    chip = t_ref[...].astype(F32)
    every, some = chip, jnp.zeros_like(chip)
    for d, g in ((1, g1), (2, g2), (3, g3)):
        value = g[...].astype(F32)
        every = every + value
        taken = first < d if reverse else first >= d
        some = some + jnp.where(taken, value, 0.0)
    own_ref[...] = some
    base = jnp.where(rows_first, 0.0, some)
    extra = jnp.where(rows_first, every, chip)
    for d, m in ((1, m1), (2, m2), (3, m3)):
        given = second + d >= 4 if reverse else second + d < 4
        m[...] = (base + jnp.where(given, extra, 0.0)).astype(BF16)


def second_axis_body(reverse, place, own_ref, g1, g2, g3, keep_ref, got_ref, out_ref, send_ref):
    total = own_ref[...]
    for g in (g1, g2, g3):
        total = total + g[...].astype(F32)
    late = place[2] == (0 if reverse else 1)
    out_ref[...] = (total + jnp.where(late, got_ref[...].astype(F32), 0.0)).astype(BF16)
    send_ref[...] = (total + jnp.where(late, 0.0, keep_ref[...])).astype(BF16)


def pick_state(place, own_ref, other_ref, b, h):
    return jnp.where(place[2] == b, own_ref[h], other_ref[h])


def each_head(width, step):
    n = width // DH

    def body(i, carry):
        for j in range(2):
            b, h = i // (n // 2), 2 * (i % (n // 2)) + j
            step(b, h, b * n + h, pl.ds(pl.multiple_of(h * DH, DH), DH))
        return carry

    lax.fori_loop(0, n, body, 0)


def intra_body(q_ref, k_ref, v_ref, scores_ref, intra_ref, q_out):
    q_out[...] = q_ref[...]
    lower = lower_mask(q_ref.shape[1])

    def step(b, h, i, s):
        raw = dot(q_ref[b, :, s], k_ref[b, :, s], 1, 1) * SCALE
        scores = jnp.where(lower, raw, 0.0).astype(BF16)
        scores_ref[i] = scores
        intra_ref[b, :, s] = dot(scores, v_ref[b, :, s], 1, 0)

    each_head(q_ref.shape[2], step)


def forward_body(place, q_ref, intra_ref, so_ref, sr_ref, normed_ref, attended_ref):
    def step(b, h, i, s):
        state = pick_state(place, so_ref, sr_ref, b, h)
        attended = intra_ref[b, :, s] + SCALE * dot(q_ref[b, :, s], state, 1, 0)
        attended_ref[b, :, s] = attended
        mean = jnp.mean(attended * attended, axis=-1, keepdims=True)
        normed_ref[b, :, s] = (attended / jnp.sqrt(mean + EPS)).astype(BF16)

    each_head(q_ref.shape[2], step)


def project_body(n_ref, w_ref, out_ref):
    width = n_ref.shape[1]

    def body(i, carry):
        for j in (2 * i, 2 * i + 1):
            cols = pl.ds(pl.multiple_of(j * width, width), width)
            out_ref[j] = dot(n_ref[...], w_ref[:, cols], 1, 0).astype(BF16)
        return carry

    lax.fori_loop(0, out_ref.shape[0] // 2, body, 0)


def half_body(first, x_ref, out_ref):
    out_ref[...] = x_ref[:, first : first + out_ref.shape[1]]


def combine_body(place, o_ref, g1, g2, own_ref, s1, s2, s3):
    me = jnp.where(place[2] == 0, place[0], place[1])
    for d, out in enumerate((own_ref, s1, s2, s3)):
        i = (me + d) % 4
        total = o_ref[i].astype(F32) + g1[i].astype(F32) + g2[i].astype(F32)
        out[...] = total.astype(out.dtype)


def finish_body(factor, own_ref, g1, g2, g3, out_ref):
    total = own_ref[...]
    for g in (g1, g2, g3):
        total = total + g[...].astype(F32)
    out_ref[...] = total * factor


def owner_of(place, step):
    return (place[3] + step + 8) % 8


def block_dot(place, step, ref, w_ref, first=0):
    width = w_ref.shape[0]
    start = pl.multiple_of(owner_of(place, step) * width + first, DH)
    return dot(ref[...], w_ref[:, pl.ds(start, ref.shape[1])], 1, 1)


def grad_near_body(steps, place, *refs):
    *blocks, w_ref, out_ref = refs
    total = block_dot(place, steps[0], blocks[0], w_ref)
    for step, ref in zip(steps[1:], blocks[1:]):
        total = total + block_dot(place, step, ref, w_ref)
    out_ref[...] = total


def grad_far_body(place, *refs):
    r4, l4, w_ref, sum_ref, a_ref, q_ref, ag_ref, keep_ref, send_ref, acc = refs
    _, width = sum_ref.shape
    half = block_dot(place, 4, r4, w_ref) + block_dot(place, 4, l4, w_ref, width // 2)
    acc[...] = (sum_ref[...] + half).reshape(acc.shape)

    def step(b, h, i, s):
        a, g = a_ref[b, :, s], acc[b, :, s]
        root = 1.0 / jnp.sqrt(jnp.mean(a * a, axis=-1, keepdims=True) + EPS)
        inner = jnp.mean(g * a, axis=-1, keepdims=True)
        ag_ref[b, :, s] = (g * root - a * (inner * root * root * root)).astype(BF16)

    each_head(width, step)
    local_states(place, q_ref, ag_ref, keep_ref, send_ref)


def weight_tiles(place, mc, step):
    mx, my = place[0], place[1]
    k = owner_of(place, step)
    x = k // 2
    for j in range(2):
        y = 2 * (k % 2) + j
        far = jnp.where(mc == 0, (y - my + 4) % 4, (x - mx + 4) % 4)
        yield far, jnp.where(mc == 0, x, y)


def weight_pair(mc, n_ref, left, right, left_at, right_at):
    low = pl.multiple_of(mc * DH + left_at, DH)
    high = pl.multiple_of(mc * DH + right_at, DH)
    both = jnp.concatenate([left[:, pl.ds(low, DH)], right[:, pl.ds(high, DH)]], axis=1)
    r = dot(n_ref[...], both, 0, 0)
    return r[:, :DH], r[:, DH:]


def weight_near_body(steps, place, n_ref, *refs):
    *blocks, out_ref = refs
    mc = 1 - place[2]
    for step, ref in zip(steps, blocks):
        pieces = weight_pair(mc, n_ref, ref, ref, 0, 2 * DH)
        for (far, other), piece in zip(weight_tiles(place, mc, step), pieces):
            out_ref[far, other] = piece.astype(BF16)
    for far, other in weight_tiles(place, mc, 4):
        out_ref[far, other] = jnp.zeros(out_ref.shape[2:], BF16)


def weight_far_body(place, n_ref, r4, l4, out_ref):
    for j, piece in enumerate(weight_pair(1 - place[2], n_ref, r4, l4, 0, 0)):
        out_ref[j] = piece.astype(BF16)


def weight_add_body(steps, place, n_ref, *refs):
    *blocks, r4, l4, near_ref, far_ref, o0, o1, low2, high2, o3, buf, sem = refs
    mc = place[2]
    for step, ref in zip(steps, blocks):
        pieces = weight_pair(mc, n_ref, ref, ref, 0, 2 * DH)
        for (far, other), piece in zip(weight_tiles(place, mc, step), pieces):
            buf[far, other] = (piece + near_ref[far, other].astype(F32)).astype(BF16)
    pieces = weight_pair(mc, n_ref, r4, l4, 0, 0)
    for j, ((far, other), piece) in enumerate(zip(weight_tiles(place, mc, 4), pieces)):
        buf[far, other] = (piece + far_ref[j].astype(F32)).astype(BF16)
    n = low2.shape[0]
    moves = [(buf.at[2, :n], low2), (buf.at[2, n:], high2)]
    moves += [(buf.at[0], o0), (buf.at[1], o1), (buf.at[3], o3)]
    copies = [pltpu.make_async_copy(a, o, sem.at[d]) for d, (a, o) in enumerate(moves)]
    for copy in copies:
        copy.start()
    for copy in copies:
        copy.wait()


def relay_body(up_ref, down_ref, from_below, from_above, up_out, down_out):
    n = from_below.shape[0]
    up_out[:n] = (up_ref[:n].astype(F32) + from_below[...].astype(F32)).astype(BF16)
    up_out[n:] = up_ref[n:]
    down_out[:n] = down_ref[:n]
    down_out[n:] = (down_ref[n:].astype(F32) + from_above[...].astype(F32)).astype(BF16)


def inner_body(place, q_ref, k_ref, v_ref, sc_ref, ag_ref, so, sr, dq_ref, dk_ref, dv_ref):
    lower = lower_mask(q_ref.shape[1])

    def step(b, h, i, s):
        ag = ag_ref[b, :, s]
        sg = jnp.where(lower, dot(ag, v_ref[b, :, s], 1, 1) * SCALE, 0.0).astype(BF16)
        earlier = pick_state(place, so, sr, b, h)
        dq_ref[b, :, s] = (dot(sg, k_ref[b, :, s], 1, 0) + SCALE * dot(ag, earlier, 1, 1)).astype(BF16)
        dk_ref[b, :, s] = dot(sg, q_ref[b, :, s], 0, 0)
        dv_ref[b, :, s] = dot(sc_ref[i], ag, 0, 0)

    each_head(q_ref.shape[2], step)


def outer_body(place, k_ref, v_ref, ik_ref, iv_ref, go, gr, dk_ref, dv_ref):
    def step(b, h, i, s):
        later = pick_state(place, go, gr, b, h)
        dk_ref[b, :, s] = (ik_ref[b, :, s] + SCALE * dot(v_ref[b, :, s], later, 1, 1)).astype(BF16)
        dv_ref[b, :, s] = (iv_ref[b, :, s] + SCALE * dot(k_ref[b, :, s], later, 1, 0)).astype(BF16)

    each_head(k_ref.shape[2], step)


def shift(value, axis, step):
    n = lax.axis_size(axis)
    return lax.ppermute(value, axis, [(i, (i + step) % n) for i in range(n)])


def shift_by_core(value, first, step):
    def target(x, y, c):
        along_y = (c == 0) == first
        return (x, (y + step) % 4, c) if along_y else ((x + step) % 4, y, c)

    def index(x, y, c):
        return (x * 4 + y) * 2 + c

    places = [(x, y, c) for x in range(4) for y in range(4) for c in range(2)]
    return lax.ppermute(value, CTX, [(index(*p), index(*target(*p))) for p in places])


def exclusive(place, keep, send, reverse):
    half, size = keep.shape, keep.size
    got = shift(send, "ctx_2", 1)
    chip = call(chip_body, [shape(half, BF16)], [keep, got], size)[0]
    near = []
    for d in (1, 2, 3):
        near.append(shift_by_core(chip, True, d))
    own, *out = call(
        functools.partial(first_axis_body, reverse),
        [shape(half, F32)] + [shape(half, BF16)] * 3,
        [place, chip, *near],
        size * 10,
        True,
    )
    far = []
    for d in (1, 2, 3):
        far.append(shift_by_core(out[d - 1], False, d))
    mine, other = call(
        functools.partial(second_axis_body, reverse),
        [shape(half, BF16)] * 2,
        [place, own, *far, keep, got],
        size * 8,
        True,
    )
    return mine, shift(other, "ctx_2", 1)


def gather_ring(block):
    near, right, left = [block], block, block
    rows, width = block.shape
    for i in (1, 2, 3, 4):
        if i == 4:
            half = [shape((rows, width // 2), BF16)]
            right = call(functools.partial(half_body, 0), half, [right], 0)[0]
            left = call(functools.partial(half_body, width // 2), half, [left], 0)[0]
        right = shift(right, "head", 1)
        left = shift(left, "head", -1)
        near += [right, left]
    return near


def send_near(place, normed, blocks):
    rows, width = normed.shape
    near = call(
        functools.partial(weight_near_body, STEPS),
        [shape((4, 4, width, DH), BF16)],
        [place, normed, *blocks[:7]],
        rows * width * width * 7,
        True,
    )[0]
    return shift(near, "ctx_2", 1)


def reduce_weight(place, normed, blocks, near, factor):
    rows, width = normed.shape
    flops = rows * width * width
    far = call(
        weight_far_body, [shape((2, width, DH), BF16)], [place, normed, *blocks[7:]], flops, True
    )[0]
    far = shift(far, "ctx_2", 1)
    whole, part = (4, width, DH), (2, width, DH)
    own, up, low, high, down = call(
        functools.partial(weight_add_body, STEPS),
        [shape(d, BF16) for d in (whole, whole, part, part, whole)],
        [place, normed, *blocks, near, far],
        flops * 8,
        True,
        [VMEM((4, *whole), BF16), pltpu.SemaphoreType.DMA((5,))],
    )
    low = shift_by_core(low, True, 1)
    high = shift_by_core(high, True, -1)
    up, down = call(relay_body, [shape(whole, BF16)] * 2, [up, down, low, high], up.size)
    up = shift_by_core(up, True, 1)
    down = shift_by_core(down, True, -1)
    piece = (width, DH)
    own, *send = call(
        combine_body,
        [shape(piece, F32)] + [shape(piece, BF16)] * 3,
        [place, own, up, down],
        own.size * 3,
        True,
    )
    got = []
    for d in (1, 2, 3):
        got.append(shift_by_core(send[d - 1], False, d))
    return call(functools.partial(finish_body, factor), [shape(piece, F32)], [own, *got], own.size * 4)[0]


def layer(queries, key_rows, value_rows, out_weight, cotangent):
    _, length, width = queries.shape
    n_head = lax.axis_size("head")
    rows = 2 * length
    n_mat = 2 * width // DH
    half = (n_mat // 2, DH, DH)
    blocks = gather_ring(cotangent.reshape(rows, width))
    mx, my, mc, mz = (lax.axis_index(a) for a in (*CTX, "head"))
    place = jnp.stack([mx, my, mc, mz]).astype(jnp.int32)
    mat_flops = 2 * n_mat * length * DH * DH
    pair = [shape(half, F32), shape(half, BF16)]
    keep, send, near_keys, near_values = call(
        state_body,
        pair + [shape(queries.shape, BF16)] * 2,
        [place, key_rows, value_rows],
        mat_flops,
        True,
    )
    scores, intra, near_queries = call(
        intra_body,
        [shape((n_mat, length, length), BF16), shape(queries.shape, F32), shape(queries.shape, BF16)],
        [queries, near_keys, near_values],
        3 * mat_flops,
    )
    state = exclusive(place, keep, send, False)
    normed, attended = call(
        forward_body,
        [shape(queries.shape, BF16), shape(queries.shape, F32)],
        [place, near_queries, intra, *state],
        mat_flops,
        True,
    )
    normed = normed.reshape(rows, width)
    big = 2 * rows * width * width * n_head
    partial = call(project_body, [shape((n_head, rows, width), BF16)], [normed, out_weight], big)[0]
    layer_output = lax.psum_scatter(
        partial.reshape(n_head * rows, width), "head", scatter_dimension=0, tiled=True
    ).reshape(queries.shape)
    near = send_near(place, normed, blocks)
    part_grad = call(
        functools.partial(grad_near_body, STEPS),
        [shape((rows, width), F32)],
        [place, *blocks[:7], out_weight],
        big * 7 // 8,
        True,
    )[0]
    attended_grad, keep, send = call(
        grad_far_body,
        [shape(queries.shape, BF16), *pair],
        [place, *blocks[7:], out_weight, part_grad, attended, queries],
        big // 8,
        True,
        [VMEM(queries.shape, F32)],
    )
    factor = (rows * lax.axis_size(CTX)) ** (-0.5)
    weight_grad = reduce_weight(place, normed, blocks, near, factor)
    grad_state = exclusive(place, keep, send, True)
    query_grad, inner_key, inner_value = call(
        inner_body,
        [shape(queries.shape, BF16)] + [shape(queries.shape, F32)] * 2,
        [place, queries, key_rows, value_rows, scores, attended_grad, *state],
        5 * mat_flops,
        True,
    )
    key_grad, value_grad = call(
        outer_body,
        [shape(queries.shape, BF16)] * 2,
        [place, key_rows, value_rows, inner_key, inner_value, *grad_state],
        2 * mat_flops,
        True,
    )
    return (layer_output, query_grad, key_grad, value_grad, weight_grad)


def solution(mesh):
    split = Mesh(
        mesh.devices.reshape(4, 4, 2, mesh.shape["head"]), ("ctx_0", "ctx_1", "ctx_2", "head")
    )
    rows = P(None, CTX, "head")
    return jax.shard_map(
        layer,
        mesh=split,
        in_specs=(rows, rows, rows, P("head", None), rows),
        out_specs=(rows, rows, rows, rows, P("head", CTX)),
        check_vma=False,
    )
```

```python
import functools

import jax
import jax.numpy as jnp
from jax import lax
from jax.experimental import pallas as pl
from jax.experimental.pallas import tpu as pltpu
from jax.sharding import Mesh
from jax.sharding import PartitionSpec as P

DH = 128
CTX = ("ctx_0", "ctx_1", "ctx_2")
SCALE = DH ** (-0.5)
EPS = 1e-06
F32, BF16 = jnp.float32, jnp.bfloat16
VMEM = pltpu.VMEM
LIMIT = 20 << 20
SMEM = pltpu.SMEM
STEPS = (0, -1, 1, -2, 2, -3, 3)


def dot(a, b, ca, cb):
    return lax.dot_general(a, b, (((ca,), (cb,)), ((), ())), preferred_element_type=F32)


def call(body, outs, args, flops, scalar=False, scratch=()):
    size = sum(a.size * a.dtype.itemsize for a in args)
    size += sum(o.size * o.dtype.itemsize for o in outs)
    cost = pl.CostEstimate(flops=flops, bytes_accessed=size, transcendentals=0)
    specs = [pl.BlockSpec(memory_space=VMEM)] * len(args)
    if scalar:
        specs[0] = pl.BlockSpec(memory_space=SMEM)
    return pl.pallas_call(
        body,
        out_shape=outs,
        in_specs=specs,
        out_specs=[pl.BlockSpec(memory_space=VMEM)] * len(outs),
        scratch_shapes=list(scratch),
        cost_estimate=cost,
        compiler_params=pltpu.CompilerParams(vmem_limit_bytes=LIMIT),
    )(*args)


def shape(dims, dtype):
    return jax.ShapeDtypeStruct(dims, dtype)


def lower_mask(n):
    return lax.broadcasted_iota(jnp.int32, (n, n), 0) >= lax.broadcasted_iota(jnp.int32, (n, n), 1)


def local_states(place, left, right, keep_ref, send_ref):
    mc = place[2]
    for h in range(keep_ref.shape[0]):
        s = slice(h * DH, (h + 1) * DH)
        keep_ref[h] = dot(left[mc, :, s], right[mc, :, s], 0, 0)
        send_ref[h] = dot(left[1 - mc, :, s], right[1 - mc, :, s], 0, 0).astype(BF16)


def state_body(place, k_ref, v_ref, keep_ref, send_ref, k_out, v_out):
    local_states(place, k_ref, v_ref, keep_ref, send_ref)
    k_out[...] = k_ref[...]
    v_out[...] = v_ref[...]


def chip_body(keep_ref, got_ref, out_ref):
    out_ref[...] = (keep_ref[...] + got_ref[...].astype(F32)).astype(BF16)


def first_axis_body(reverse, place, t_ref, g1, g2, g3, own_ref, m1, m2, m3):
    rows_first = place[2] == 0
    first = jnp.where(rows_first, place[1], place[0])
    second = jnp.where(rows_first, place[0], place[1])
    chip = t_ref[...].astype(F32)
    every, some = chip, jnp.zeros_like(chip)
    for d, g in ((1, g1), (2, g2), (3, g3)):
        value = g[...].astype(F32)
        every = every + value
        taken = first < d if reverse else first >= d
        some = some + jnp.where(taken, value, 0.0)
    own_ref[...] = some
    base = jnp.where(rows_first, 0.0, some)
    extra = jnp.where(rows_first, every, chip)
    for d, m in ((1, m1), (2, m2), (3, m3)):
        given = second + d >= 4 if reverse else second + d < 4
        m[...] = (base + jnp.where(given, extra, 0.0)).astype(BF16)


def second_axis_body(reverse, place, own_ref, g1, g2, g3, keep_ref, got_ref, out_ref, send_ref):
    total = own_ref[...]
    for g in (g1, g2, g3):
        total = total + g[...].astype(F32)
    late = place[2] == (0 if reverse else 1)
    out_ref[...] = (total + jnp.where(late, got_ref[...].astype(F32), 0.0)).astype(BF16)
    send_ref[...] = (total + jnp.where(late, 0.0, keep_ref[...])).astype(BF16)


def pick_state(place, own_ref, other_ref, b, h):
    return jnp.where(place[2] == b, own_ref[h], other_ref[h])


def each_head(width, step):
    n = width // DH

    def body(i, carry):
        for j in range(2):
            b, h = i // (n // 2), 2 * (i % (n // 2)) + j
            step(b, h, b * n + h, pl.ds(pl.multiple_of(h * DH, DH), DH))
        return carry

    lax.fori_loop(0, n, body, 0)


def each_batch(width, step):
    def body(b, carry):
        for h in range(width // DH):
            step(b, h, b * (width // DH) + h, slice(h * DH, (h + 1) * DH))
        return carry

    lax.fori_loop(0, 2, body, 0)


def intra_body(q_ref, k_ref, v_ref, scores_ref, intra_ref, q_out):
    q_out[...] = q_ref[...]
    lower = lower_mask(q_ref.shape[1])

    def step(b, h, i, s):
        raw = dot(q_ref[b, :, s], k_ref[b, :, s], 1, 1) * SCALE
        scores = jnp.where(lower, raw, 0.0).astype(BF16)
        scores_ref[i] = scores
        intra_ref[b, :, s] = dot(scores, v_ref[b, :, s], 1, 0)

    each_head(q_ref.shape[2], step)


def forward_body(place, q_ref, intra_ref, so_ref, sr_ref, normed_ref, attended_ref):
    def step(b, h, i, s):
        state = pick_state(place, so_ref, sr_ref, b, h)
        attended = intra_ref[b, :, s] + SCALE * dot(q_ref[b, :, s], state, 1, 0)
        attended_ref[b, :, s] = attended
        mean = jnp.mean(attended * attended, axis=-1, keepdims=True)
        normed_ref[b, :, s] = (attended / jnp.sqrt(mean + EPS)).astype(BF16)

    each_head(q_ref.shape[2], step)


def project_body(n_ref, w_ref, out_ref):
    width = n_ref.shape[1]

    def body(i, carry):
        for j in (2 * i, 2 * i + 1):
            cols = pl.ds(pl.multiple_of(j * width, width), width)
            out_ref[j] = dot(n_ref[...], w_ref[:, cols], 1, 0).astype(BF16)
        return carry

    lax.fori_loop(0, out_ref.shape[0] // 2, body, 0)


def half_body(first, x_ref, out_ref):
    out_ref[...] = x_ref[:, first : first + out_ref.shape[1]]


def combine_body(place, o_ref, g1, g2, g3, own_ref, s1, s2, s3):
    me = jnp.where(place[2] == 0, place[0], place[1])
    for d, out in enumerate((own_ref, s1, s2, s3)):
        i = (me + d) % 4
        total = o_ref[i].astype(F32)
        for g in (g1, g2, g3):
            total = total + g[i].astype(F32)
        out[...] = total.astype(out.dtype)


def finish_body(factor, own_ref, g1, g2, g3, out_ref):
    total = own_ref[...]
    for g in (g1, g2, g3):
        total = total + g[...].astype(F32)
    out_ref[...] = total * factor


def owner_of(place, step):
    return (place[3] + step + 8) % 8


def block_dot(place, step, ref, w_ref, first=0):
    width = w_ref.shape[0]
    start = pl.multiple_of(owner_of(place, step) * width + first, DH)
    return dot(ref[...], w_ref[:, pl.ds(start, ref.shape[1])], 1, 1)


def grad_near_body(steps, place, *refs):
    *blocks, w_ref, out_ref = refs
    total = block_dot(place, steps[0], blocks[0], w_ref)
    for step, ref in zip(steps[1:], blocks[1:]):
        total = total + block_dot(place, step, ref, w_ref)
    out_ref[...] = total


def grad_far_body(place, *refs):
    r4, l4, w_ref, sum_ref, a_ref, q_ref, ag_ref, keep_ref, send_ref, acc = refs
    _, width = sum_ref.shape
    half = block_dot(place, 4, r4, w_ref) + block_dot(place, 4, l4, w_ref, width // 2)
    acc[...] = (sum_ref[...] + half).reshape(acc.shape)

    def step(b, h, i, s):
        a, g = a_ref[b, :, s], acc[b, :, s]
        root = 1.0 / jnp.sqrt(jnp.mean(a * a, axis=-1, keepdims=True) + EPS)
        inner = jnp.mean(g * a, axis=-1, keepdims=True)
        ag_ref[b, :, s] = (g * root - a * (inner * root * root * root)).astype(BF16)

    each_head(width, step)
    local_states(place, q_ref, ag_ref, keep_ref, send_ref)


def weight_tiles(place, mc, step):
    mx, my = place[0], place[1]
    k = owner_of(place, step)
    x = k // 2
    for j in range(2):
        y = 2 * (k % 2) + j
        far = jnp.where(mc == 0, (y - my + 4) % 4, (x - mx + 4) % 4)
        yield far, jnp.where(mc == 0, x, y)


def weight_pair(mc, n_ref, left, right, left_at, right_at):
    low = pl.multiple_of(mc * DH + left_at, DH)
    high = pl.multiple_of(mc * DH + right_at, DH)
    both = jnp.concatenate([left[:, pl.ds(low, DH)], right[:, pl.ds(high, DH)]], axis=1)
    r = dot(n_ref[...], both, 0, 0)
    return r[:, :DH], r[:, DH:]


def weight_near_body(steps, place, n_ref, *refs):
    *blocks, out_ref = refs
    mc = 1 - place[2]
    for step, ref in zip(steps, blocks):
        pieces = weight_pair(mc, n_ref, ref, ref, 0, 2 * DH)
        for (far, other), piece in zip(weight_tiles(place, mc, step), pieces):
            out_ref[far, other] = piece.astype(BF16)
    for far, other in weight_tiles(place, mc, 4):
        out_ref[far, other] = jnp.zeros(out_ref.shape[2:], BF16)


def weight_far_body(place, n_ref, r4, l4, out_ref):
    for j, piece in enumerate(weight_pair(1 - place[2], n_ref, r4, l4, 0, 0)):
        out_ref[j] = piece.astype(BF16)


def weight_add_body(steps, place, n_ref, *refs):
    *blocks, r4, l4, near_ref, far_ref, o0, o1, o2, o3, buf, sem = refs
    mc = place[2]
    for step, ref in zip(steps, blocks):
        pieces = weight_pair(mc, n_ref, ref, ref, 0, 2 * DH)
        for (far, other), piece in zip(weight_tiles(place, mc, step), pieces):
            buf[far, other] = (piece + near_ref[far, other].astype(F32)).astype(BF16)
    pieces = weight_pair(mc, n_ref, r4, l4, 0, 0)
    for j, ((far, other), piece) in enumerate(zip(weight_tiles(place, mc, 4), pieces)):
        buf[far, other] = (piece + far_ref[j].astype(F32)).astype(BF16)
    copies = [
        pltpu.make_async_copy(buf.at[d], o, sem.at[d]) for d, o in enumerate((o0, o1, o2, o3))
    ]
    for copy in copies:
        copy.start()
    for copy in copies:
        copy.wait()


def inner_body(place, q_ref, k_ref, v_ref, sc_ref, ag_ref, so, sr, dq_ref, dk_ref, dv_ref):
    lower = lower_mask(q_ref.shape[1])

    def step(b, h, i, s):
        ag = ag_ref[b, :, s]
        sg = jnp.where(lower, dot(ag, v_ref[b, :, s], 1, 1) * SCALE, 0.0).astype(BF16)
        earlier = pick_state(place, so, sr, b, h)
        dq_ref[b, :, s] = (dot(sg, k_ref[b, :, s], 1, 0) + SCALE * dot(ag, earlier, 1, 1)).astype(BF16)
        dk_ref[b, :, s] = dot(sg, q_ref[b, :, s], 0, 0)
        dv_ref[b, :, s] = dot(sc_ref[i], ag, 0, 0)

    each_batch(q_ref.shape[2], step)


def outer_body(place, k_ref, v_ref, ik_ref, iv_ref, go, gr, dk_ref, dv_ref):
    def step(b, h, i, s):
        later = pick_state(place, go, gr, b, h)
        dk_ref[b, :, s] = (ik_ref[b, :, s] + SCALE * dot(v_ref[b, :, s], later, 1, 1)).astype(BF16)
        dv_ref[b, :, s] = (iv_ref[b, :, s] + SCALE * dot(k_ref[b, :, s], later, 1, 0)).astype(BF16)

    each_head(k_ref.shape[2], step)


def shift(value, axis, step):
    n = lax.axis_size(axis)
    return lax.ppermute(value, axis, [(i, (i + step) % n) for i in range(n)])


def shift_by_core(value, first, step):
    def target(x, y, c):
        along_y = (c == 0) == first
        return (x, (y + step) % 4, c) if along_y else ((x + step) % 4, y, c)

    def index(x, y, c):
        return (x * 4 + y) * 2 + c

    places = [(x, y, c) for x in range(4) for y in range(4) for c in range(2)]
    return lax.ppermute(value, CTX, [(index(*p), index(*target(*p))) for p in places])


def exclusive(place, keep, send, reverse):
    half, size = keep.shape, keep.size
    got = shift(send, "ctx_2", 1)
    chip = call(chip_body, [shape(half, BF16)], [keep, got], size)[0]
    near = []
    for d in (1, 2, 3):
        near.append(shift_by_core(chip, True, d))
    own, *out = call(
        functools.partial(first_axis_body, reverse),
        [shape(half, F32)] + [shape(half, BF16)] * 3,
        [place, chip, *near],
        size * 10,
        True,
    )
    far = []
    for d in (1, 2, 3):
        far.append(shift_by_core(out[d - 1], False, d))
    mine, other = call(
        functools.partial(second_axis_body, reverse),
        [shape(half, BF16)] * 2,
        [place, own, *far, keep, got],
        size * 8,
        True,
    )
    return mine, shift(other, "ctx_2", 1)


def gather_ring(block):
    near, right, left = [block], block, block
    rows, width = block.shape
    for i in (1, 2, 3, 4):
        if i == 4:
            half = [shape((rows, width // 2), BF16)]
            right = call(functools.partial(half_body, 0), half, [right], 0)[0]
            left = call(functools.partial(half_body, width // 2), half, [left], 0)[0]
        right = shift(right, "head", 1)
        left = shift(left, "head", -1)
        near += [right, left]
    return near


def send_near(place, normed, blocks):
    rows, width = normed.shape
    near = call(
        functools.partial(weight_near_body, STEPS),
        [shape((4, 4, width, DH), BF16)],
        [place, normed, *blocks[:7]],
        rows * width * width * 7,
        True,
    )[0]
    return shift(near, "ctx_2", 1)


def reduce_weight(place, normed, blocks, near, factor):
    rows, width = normed.shape
    flops = rows * width * width
    far = call(
        weight_far_body, [shape((2, width, DH), BF16)], [place, normed, *blocks[7:]], flops, True
    )[0]
    far = shift(far, "ctx_2", 1)
    whole = (4, width, DH)
    own, *send = call(
        functools.partial(weight_add_body, STEPS),
        [shape(whole, BF16)] * 4,
        [place, normed, *blocks, near, far],
        flops * 8,
        True,
        [VMEM((4, *whole), BF16), pltpu.SemaphoreType.DMA((4,))],
    )
    got = []
    for d in (1, 2, 3):
        got.append(shift_by_core(send[d - 1], True, d))
    piece = (width, DH)
    own, *send = call(
        combine_body,
        [shape(piece, F32)] + [shape(piece, BF16)] * 3,
        [place, own, *got],
        own.size * 4,
        True,
    )
    got = []
    for d in (1, 2, 3):
        got.append(shift_by_core(send[d - 1], False, d))
    return call(functools.partial(finish_body, factor), [shape(piece, F32)], [own, *got], own.size * 4)[0]


def layer(queries, key_rows, value_rows, out_weight, cotangent):
    _, length, width = queries.shape
    n_head = lax.axis_size("head")
    rows = 2 * length
    n_mat = 2 * width // DH
    half = (n_mat // 2, DH, DH)
    blocks = gather_ring(cotangent.reshape(rows, width))
    mx, my, mc, mz = (lax.axis_index(a) for a in (*CTX, "head"))
    place = jnp.stack([mx, my, mc, mz]).astype(jnp.int32)
    mat_flops = 2 * n_mat * length * DH * DH
    pair = [shape(half, F32), shape(half, BF16)]
    keep, send, near_keys, near_values = call(
        state_body,
        pair + [shape(queries.shape, BF16)] * 2,
        [place, key_rows, value_rows],
        mat_flops,
        True,
    )
    scores, intra, near_queries = call(
        intra_body,
        [shape((n_mat, length, length), BF16), shape(queries.shape, F32), shape(queries.shape, BF16)],
        [queries, near_keys, near_values],
        3 * mat_flops,
    )
    state = exclusive(place, keep, send, False)
    normed, attended = call(
        forward_body,
        [shape(queries.shape, BF16), shape(queries.shape, F32)],
        [place, near_queries, intra, *state],
        mat_flops,
        True,
    )
    normed = normed.reshape(rows, width)
    big = 2 * rows * width * width * n_head
    partial = call(project_body, [shape((n_head, rows, width), BF16)], [normed, out_weight], big)[0]
    layer_output = lax.psum_scatter(
        partial.reshape(n_head * rows, width), "head", scatter_dimension=0, tiled=True
    ).reshape(queries.shape)
    near = send_near(place, normed, blocks)
    part_grad = call(
        functools.partial(grad_near_body, STEPS),
        [shape((rows, width), F32)],
        [place, *blocks[:7], out_weight],
        big * 7 // 8,
        True,
    )[0]
    attended_grad, keep, send = call(
        grad_far_body,
        [shape(queries.shape, BF16), *pair],
        [place, *blocks[7:], out_weight, part_grad, attended, queries],
        big // 8,
        True,
        [VMEM(queries.shape, F32)],
    )
    factor = (rows * lax.axis_size(CTX)) ** (-0.5)
    weight_grad = reduce_weight(place, normed, blocks, near, factor)
    grad_state = exclusive(place, keep, send, True)
    query_grad, inner_key, inner_value = call(
        inner_body,
        [shape(queries.shape, BF16)] + [shape(queries.shape, F32)] * 2,
        [place, queries, key_rows, value_rows, scores, attended_grad, *state],
        5 * mat_flops,
        True,
    )
    key_grad, value_grad = call(
        outer_body,
        [shape(queries.shape, BF16)] * 2,
        [place, key_rows, value_rows, inner_key, inner_value, *grad_state],
        2 * mat_flops,
        True,
    )
    return (layer_output, query_grad, key_grad, value_grad, weight_grad)


def solution(mesh):
    split = Mesh(
        mesh.devices.reshape(4, 4, 2, mesh.shape["head"]), ("ctx_0", "ctx_1", "ctx_2", "head")
    )
    rows = P(None, CTX, "head")
    return jax.shard_map(
        layer,
        mesh=split,
        in_specs=(rows, rows, rows, P("head", None), rows),
        out_specs=(rows, rows, rows, rows, P("head", CTX)),
        check_vma=False,
    )
```

```python
import functools

import jax
import jax.numpy as jnp
from jax import lax
from jax.experimental import pallas as pl
from jax.experimental.pallas import tpu as pltpu
from jax.sharding import Mesh
from jax.sharding import PartitionSpec as P

DH = 128
CTX = ("ctx_0", "ctx_1", "ctx_2")
SCALE = DH ** (-0.5)
EPS = 1e-06
F32, BF16 = jnp.float32, jnp.bfloat16
VMEM = pltpu.VMEM
LIMIT = 20 << 20
SMEM = pltpu.SMEM
STEPS = (0, -1, 1, -2, 2, -3, 3)


def dot(a, b, ca, cb):
    return lax.dot_general(a, b, (((ca,), (cb,)), ((), ())), preferred_element_type=F32)


def call(body, outs, args, flops, scalar=False, scratch=(), last=VMEM):
    size = sum(a.size * a.dtype.itemsize for a in args)
    size += sum(o.size * o.dtype.itemsize for o in outs)
    cost = pl.CostEstimate(flops=flops, bytes_accessed=size, transcendentals=0)
    specs = [pl.BlockSpec(memory_space=VMEM)] * len(args)
    specs[-1] = pl.BlockSpec(memory_space=last)
    if scalar:
        specs[0] = pl.BlockSpec(memory_space=SMEM)
    return pl.pallas_call(
        body,
        out_shape=outs,
        in_specs=specs,
        out_specs=[pl.BlockSpec(memory_space=VMEM)] * len(outs),
        scratch_shapes=list(scratch),
        cost_estimate=cost,
        compiler_params=pltpu.CompilerParams(vmem_limit_bytes=LIMIT),
    )(*args)


def shape(dims, dtype):
    return jax.ShapeDtypeStruct(dims, dtype)


def lower_mask(n):
    return lax.broadcasted_iota(jnp.int32, (n, n), 0) >= lax.broadcasted_iota(jnp.int32, (n, n), 1)


def local_states(place, left, right, keep_ref, send_ref):
    mc = place[2]
    for h in range(keep_ref.shape[0]):
        s = slice(h * DH, (h + 1) * DH)
        keep_ref[h] = dot(left[mc, :, s], right[mc, :, s], 0, 0)
        send_ref[h] = dot(left[1 - mc, :, s], right[1 - mc, :, s], 0, 0).astype(BF16)


def state_body(place, k_ref, v_ref, q_hbm, keep_ref, send_ref, k_out, v_out, q_out, sem):
    copy = pltpu.make_async_copy(q_hbm, q_out, sem)
    copy.start()
    local_states(place, k_ref, v_ref, keep_ref, send_ref)
    k_out[...] = k_ref[...]
    v_out[...] = v_ref[...]
    copy.wait()


def chip_body(keep_ref, got_ref, out_ref):
    out_ref[...] = (keep_ref[...] + got_ref[...].astype(F32)).astype(BF16)


def first_axis_body(reverse, place, t_ref, g1, g2, g3, own_ref, m1, m2, m3):
    rows_first = place[2] == 0
    first = jnp.where(rows_first, place[1], place[0])
    second = jnp.where(rows_first, place[0], place[1])
    chip = t_ref[...].astype(F32)
    every, some = chip, jnp.zeros_like(chip)
    for d, g in ((1, g1), (2, g2), (3, g3)):
        value = g[...].astype(F32)
        every = every + value
        taken = first < d if reverse else first >= d
        some = some + jnp.where(taken, value, 0.0)
    own_ref[...] = some
    base = jnp.where(rows_first, 0.0, some)
    extra = jnp.where(rows_first, every, chip)
    for d, m in ((1, m1), (2, m2), (3, m3)):
        given = second + d >= 4 if reverse else second + d < 4
        m[...] = (base + jnp.where(given, extra, 0.0)).astype(BF16)


def second_axis_body(reverse, place, own_ref, g1, g2, g3, keep_ref, got_ref, out_ref, send_ref):
    total = own_ref[...]
    for g in (g1, g2, g3):
        total = total + g[...].astype(F32)
    late = place[2] == (0 if reverse else 1)
    out_ref[...] = (total + jnp.where(late, got_ref[...].astype(F32), 0.0)).astype(BF16)
    send_ref[...] = (total + jnp.where(late, 0.0, keep_ref[...])).astype(BF16)


def pick_state(place, own_ref, other_ref, b, h):
    return jnp.where(place[2] == b, own_ref[h], other_ref[h])


def each_head(width, step):
    n = width // DH

    def body(i, carry):
        for j in range(2):
            b, h = i // (n // 2), 2 * (i % (n // 2)) + j
            step(b, h, b * n + h, pl.ds(pl.multiple_of(h * DH, DH), DH))
        return carry

    lax.fori_loop(0, n, body, 0)


def each_batch(width, step):
    def body(b, carry):
        for h in range(width // DH):
            step(b, h, b * (width // DH) + h, slice(h * DH, (h + 1) * DH))
        return carry

    lax.fori_loop(0, 2, body, 0)


def masked_scores(lower, left, right):
    return jnp.where(lower, dot(left, right, 1, 1) * SCALE, 0.0).astype(BF16)


def intra_body(q_ref, k_ref, v_ref, intra_ref):
    lower = lower_mask(q_ref.shape[1])

    def step(b, h, i, s):
        scores = masked_scores(lower, q_ref[b, :, s], k_ref[b, :, s])
        intra_ref[b, :, s] = dot(scores, v_ref[b, :, s], 1, 0)

    each_batch(q_ref.shape[2], step)


def forward_body(place, q_ref, intra_ref, so_ref, sr_ref, normed_ref, attended_ref):
    def step(b, h, i, s):
        state = pick_state(place, so_ref, sr_ref, b, h)
        attended = intra_ref[b, :, s] + SCALE * dot(q_ref[b, :, s], state, 1, 0)
        attended_ref[b, :, s] = attended
        mean = jnp.mean(attended * attended, axis=-1, keepdims=True)
        normed_ref[b, :, s] = (attended / jnp.sqrt(mean + EPS)).astype(BF16)

    each_head(q_ref.shape[2], step)


def project_body(n_ref, w_ref, out_ref):
    width = n_ref.shape[1]

    def body(i, carry):
        for j in (2 * i, 2 * i + 1):
            cols = pl.ds(pl.multiple_of(j * width, width), width)
            out_ref[j] = dot(n_ref[...], w_ref[:, cols], 1, 0).astype(BF16)
        return carry

    lax.fori_loop(0, out_ref.shape[0] // 2, body, 0)


def half_body(first, x_ref, out_ref):
    out_ref[...] = x_ref[:, first : first + out_ref.shape[1]]


def combine_body(place, o_ref, g1, g2, g3, own_ref, s1, s2, s3):
    me = jnp.where(place[2] == 0, place[0], place[1])
    for d, out in enumerate((own_ref, s1, s2, s3)):
        i = (me + d) % 4
        total = o_ref[i].astype(F32)
        for g in (g1, g2, g3):
            total = total + g[i].astype(F32)
        out[...] = total.astype(out.dtype)


def finish_body(factor, own_ref, g1, g2, g3, out_ref):
    total = own_ref[...]
    for g in (g1, g2, g3):
        total = total + g[...].astype(F32)
    out_ref[...] = total * factor


def owner_of(place, step):
    return (place[3] + step + 8) % 8


def block_dot(place, step, ref, w_ref, first=0):
    width = w_ref.shape[0]
    start = pl.multiple_of(owner_of(place, step) * width + first, DH)
    return dot(ref[...], w_ref[:, pl.ds(start, ref.shape[1])], 1, 1)


def grad_near_body(steps, place, *refs):
    *blocks, w_ref, out_ref = refs
    total = block_dot(place, steps[0], blocks[0], w_ref)
    for step, ref in zip(steps[1:], blocks[1:]):
        total = total + block_dot(place, step, ref, w_ref)
    out_ref[...] = total


def grad_far_body(place, *refs):
    r4, l4, w_ref, sum_ref, a_ref, q_ref, ag_ref, keep_ref, send_ref, acc = refs
    _, width = sum_ref.shape
    half = block_dot(place, 4, r4, w_ref) + block_dot(place, 4, l4, w_ref, width // 2)
    acc[...] = (sum_ref[...] + half).reshape(acc.shape)

    def step(b, h, i, s):
        a, g = a_ref[b, :, s], acc[b, :, s]
        root = 1.0 / jnp.sqrt(jnp.mean(a * a, axis=-1, keepdims=True) + EPS)
        inner = jnp.mean(g * a, axis=-1, keepdims=True)
        ag_ref[b, :, s] = (g * root - a * (inner * root * root * root)).astype(BF16)

    each_head(width, step)
    local_states(place, q_ref, ag_ref, keep_ref, send_ref)


def weight_tiles(place, mc, step):
    mx, my = place[0], place[1]
    k = owner_of(place, step)
    x = k // 2
    for j in range(2):
        y = 2 * (k % 2) + j
        far = jnp.where(mc == 0, (y - my + 4) % 4, (x - mx + 4) % 4)
        yield far, jnp.where(mc == 0, x, y)


def weight_pair(mc, n_ref, left, right, left_at, right_at):
    low = pl.multiple_of(mc * DH + left_at, DH)
    high = pl.multiple_of(mc * DH + right_at, DH)
    both = jnp.concatenate([left[:, pl.ds(low, DH)], right[:, pl.ds(high, DH)]], axis=1)
    r = dot(n_ref[...], both, 0, 0)
    return r[:, :DH], r[:, DH:]


def weight_near_body(steps, place, n_ref, *refs):
    *blocks, out_ref = refs
    mc = 1 - place[2]
    for step, ref in zip(steps, blocks):
        pieces = weight_pair(mc, n_ref, ref, ref, 0, 2 * DH)
        for (far, other), piece in zip(weight_tiles(place, mc, step), pieces):
            out_ref[far, other] = piece.astype(BF16)
    for far, other in weight_tiles(place, mc, 4):
        out_ref[far, other] = jnp.zeros(out_ref.shape[2:], BF16)


def weight_far_body(place, n_ref, r4, l4, out_ref):
    for j, piece in enumerate(weight_pair(1 - place[2], n_ref, r4, l4, 0, 0)):
        out_ref[j] = piece.astype(BF16)


def weight_add_body(steps, place, n_ref, *refs):
    *blocks, r4, l4, near_ref, far_ref, o0, o1, o2, o3, buf, sem = refs
    mc = place[2]
    for step, ref in zip(steps, blocks):
        pieces = weight_pair(mc, n_ref, ref, ref, 0, 2 * DH)
        for (far, other), piece in zip(weight_tiles(place, mc, step), pieces):
            buf[far, other] = (piece + near_ref[far, other].astype(F32)).astype(BF16)
    pieces = weight_pair(mc, n_ref, r4, l4, 0, 0)
    for j, ((far, other), piece) in enumerate(zip(weight_tiles(place, mc, 4), pieces)):
        buf[far, other] = (piece + far_ref[j].astype(F32)).astype(BF16)
    copies = [
        pltpu.make_async_copy(buf.at[d], o, sem.at[d]) for d, o in enumerate((o0, o1, o2, o3))
    ]
    for copy in copies:
        copy.start()
    for copy in copies:
        copy.wait()


def inner_body(place, q_ref, k_ref, v_ref, ag_ref, so, sr, dq_ref, dk_ref, dv_ref):
    lower = lower_mask(q_ref.shape[1])

    def step(b, h, i, s):
        ag = ag_ref[b, :, s]
        sg = masked_scores(lower, ag, v_ref[b, :, s])
        scores = masked_scores(lower, q_ref[b, :, s], k_ref[b, :, s])
        earlier = pick_state(place, so, sr, b, h)
        dq_ref[b, :, s] = (dot(sg, k_ref[b, :, s], 1, 0) + SCALE * dot(ag, earlier, 1, 1)).astype(BF16)
        dk_ref[b, :, s] = dot(sg, q_ref[b, :, s], 0, 0)
        dv_ref[b, :, s] = dot(scores, ag, 0, 0)

    each_batch(q_ref.shape[2], step)


def outer_body(place, k_ref, v_ref, ik_ref, iv_ref, go, gr, dk_ref, dv_ref):
    def step(b, h, i, s):
        later = pick_state(place, go, gr, b, h)
        dk_ref[b, :, s] = (ik_ref[b, :, s] + SCALE * dot(v_ref[b, :, s], later, 1, 1)).astype(BF16)
        dv_ref[b, :, s] = (iv_ref[b, :, s] + SCALE * dot(k_ref[b, :, s], later, 1, 0)).astype(BF16)

    each_head(k_ref.shape[2], step)


def shift(value, axis, step):
    n = lax.axis_size(axis)
    return lax.ppermute(value, axis, [(i, (i + step) % n) for i in range(n)])


def shift_by_core(value, first, step):
    def target(x, y, c):
        along_y = (c == 0) == first
        return (x, (y + step) % 4, c) if along_y else ((x + step) % 4, y, c)

    def index(x, y, c):
        return (x * 4 + y) * 2 + c

    places = [(x, y, c) for x in range(4) for y in range(4) for c in range(2)]
    return lax.ppermute(value, CTX, [(index(*p), index(*target(*p))) for p in places])


def exclusive(place, keep, send, reverse):
    half, size = keep.shape, keep.size
    got = shift(send, "ctx_2", 1)
    chip = call(chip_body, [shape(half, BF16)], [keep, got], size)[0]
    near = []
    for d in (1, 2, 3):
        near.append(shift_by_core(chip, True, d))
    own, *out = call(
        functools.partial(first_axis_body, reverse),
        [shape(half, F32)] + [shape(half, BF16)] * 3,
        [place, chip, *near],
        size * 10,
        True,
    )
    far = []
    for d in (1, 2, 3):
        far.append(shift_by_core(out[d - 1], False, d))
    mine, other = call(
        functools.partial(second_axis_body, reverse),
        [shape(half, BF16)] * 2,
        [place, own, *far, keep, got],
        size * 8,
        True,
    )
    return mine, shift(other, "ctx_2", 1)


def gather_ring(block):
    near, right, left = [block], block, block
    rows, width = block.shape
    for i in (1, 2, 3, 4):
        if i == 4:
            half = [shape((rows, width // 2), BF16)]
            right = call(functools.partial(half_body, 0), half, [right], 0)[0]
            left = call(functools.partial(half_body, width // 2), half, [left], 0)[0]
        right = shift(right, "head", 1)
        left = shift(left, "head", -1)
        near += [right, left]
    return near


def send_near(place, normed, blocks):
    rows, width = normed.shape
    near = call(
        functools.partial(weight_near_body, STEPS),
        [shape((4, 4, width, DH), BF16)],
        [place, normed, *blocks[:7]],
        rows * width * width * 7,
        True,
    )[0]
    return shift(near, "ctx_2", 1)


def reduce_weight(place, normed, blocks, near, factor):
    rows, width = normed.shape
    flops = rows * width * width
    far = call(
        weight_far_body, [shape((2, width, DH), BF16)], [place, normed, *blocks[7:]], flops, True
    )[0]
    far = shift(far, "ctx_2", 1)
    whole = (4, width, DH)
    own, *send = call(
        functools.partial(weight_add_body, STEPS),
        [shape(whole, BF16)] * 4,
        [place, normed, *blocks, near, far],
        flops * 8,
        True,
        [VMEM((4, *whole), BF16), pltpu.SemaphoreType.DMA((4,))],
    )
    got = []
    for d in (1, 2, 3):
        got.append(shift_by_core(send[d - 1], True, d))
    piece = (width, DH)
    own, *send = call(
        combine_body,
        [shape(piece, F32)] + [shape(piece, BF16)] * 3,
        [place, own, *got],
        own.size * 4,
        True,
    )
    got = []
    for d in (1, 2, 3):
        got.append(shift_by_core(send[d - 1], False, d))
    return call(functools.partial(finish_body, factor), [shape(piece, F32)], [own, *got], own.size * 4)[0]


def layer(queries, key_rows, value_rows, out_weight, cotangent):
    _, length, width = queries.shape
    n_head = lax.axis_size("head")
    rows = 2 * length
    n_mat = 2 * width // DH
    half = (n_mat // 2, DH, DH)
    blocks = gather_ring(cotangent.reshape(rows, width))
    mx, my, mc, mz = (lax.axis_index(a) for a in (*CTX, "head"))
    place = jnp.stack([mx, my, mc, mz]).astype(jnp.int32)
    mat_flops = 2 * n_mat * length * DH * DH
    pair = [shape(half, F32), shape(half, BF16)]
    keep, send, near_keys, near_values, near_queries = call(
        state_body,
        pair + [shape(queries.shape, BF16)] * 3,
        [place, key_rows, value_rows, queries],
        mat_flops,
        True,
        [pltpu.SemaphoreType.DMA],
        pltpu.HBM,
    )
    intra = call(
        intra_body,
        [shape(queries.shape, F32)],
        [near_queries, near_keys, near_values],
        3 * mat_flops,
    )[0]
    state = exclusive(place, keep, send, False)
    normed, attended = call(
        forward_body,
        [shape(queries.shape, BF16), shape(queries.shape, F32)],
        [place, near_queries, intra, *state],
        mat_flops,
        True,
    )
    normed = normed.reshape(rows, width)
    big = 2 * rows * width * width * n_head
    partial = call(project_body, [shape((n_head, rows, width), BF16)], [normed, out_weight], big)[0]
    layer_output = lax.psum_scatter(
        partial.reshape(n_head * rows, width), "head", scatter_dimension=0, tiled=True
    ).reshape(queries.shape)
    near = send_near(place, normed, blocks)
    part_grad = call(
        functools.partial(grad_near_body, STEPS),
        [shape((rows, width), F32)],
        [place, *blocks[:7], out_weight],
        big * 7 // 8,
        True,
    )[0]
    attended_grad, keep, send = call(
        grad_far_body,
        [shape(queries.shape, BF16), *pair],
        [place, *blocks[7:], out_weight, part_grad, attended, queries],
        big // 8,
        True,
        [VMEM(queries.shape, F32)],
    )
    factor = (rows * lax.axis_size(CTX)) ** (-0.5)
    weight_grad = reduce_weight(place, normed, blocks, near, factor)
    grad_state = exclusive(place, keep, send, True)
    query_grad, inner_key, inner_value = call(
        inner_body,
        [shape(queries.shape, BF16)] + [shape(queries.shape, F32)] * 2,
        [place, queries, key_rows, value_rows, attended_grad, *state],
        5 * mat_flops,
        True,
    )
    key_grad, value_grad = call(
        outer_body,
        [shape(queries.shape, BF16)] * 2,
        [place, key_rows, value_rows, inner_key, inner_value, *grad_state],
        2 * mat_flops,
        True,
    )
    return (layer_output, query_grad, key_grad, value_grad, weight_grad)


def solution(mesh):
    split = Mesh(
        mesh.devices.reshape(4, 4, 2, mesh.shape["head"]), ("ctx_0", "ctx_1", "ctx_2", "head")
    )
    rows = P(None, CTX, "head")
    return jax.shard_map(
        layer,
        mesh=split,
        in_specs=(rows, rows, rows, P("head", None), rows),
        out_specs=(rows, rows, rows, rows, P("head", CTX)),
        check_vma=False,
    )
```

```python
import functools

import jax
import jax.numpy as jnp
from jax import lax
from jax.experimental import pallas as pl
from jax.experimental.pallas import tpu as pltpu
from jax.sharding import Mesh
from jax.sharding import PartitionSpec as P

DH = 128
CTX = ("ctx_0", "ctx_1", "ctx_2")
SCALE = DH ** (-0.5)
EPS = 1e-06
F32, BF16 = jnp.float32, jnp.bfloat16
VMEM = pltpu.VMEM
LIMIT = 20 << 20
SMEM = pltpu.SMEM
STEPS = (0, -1, 1, -2, 2, -3, 3)


def dot(a, b, ca, cb):
    return lax.dot_general(a, b, (((ca,), (cb,)), ((), ())), preferred_element_type=F32)


def call(body, outs, args, flops, scalar=False, scratch=(), last=VMEM, result=VMEM):
    size = sum(a.size * a.dtype.itemsize for a in args)
    size += sum(o.size * o.dtype.itemsize for o in outs)
    cost = pl.CostEstimate(flops=flops, bytes_accessed=size, transcendentals=0)
    specs = [pl.BlockSpec(memory_space=VMEM)] * len(args)
    specs[-1] = pl.BlockSpec(memory_space=last)
    if scalar:
        specs[0] = pl.BlockSpec(memory_space=SMEM)
    return pl.pallas_call(
        body,
        out_shape=outs,
        in_specs=specs,
        out_specs=[pl.BlockSpec(memory_space=result)] * len(outs),
        scratch_shapes=list(scratch),
        cost_estimate=cost,
        compiler_params=pltpu.CompilerParams(vmem_limit_bytes=LIMIT),
    )(*args)


def shape(dims, dtype):
    return jax.ShapeDtypeStruct(dims, dtype)


def lower_mask(n):
    return lax.broadcasted_iota(jnp.int32, (n, n), 0) >= lax.broadcasted_iota(jnp.int32, (n, n), 1)


def local_states(place, left, right, keep_ref, send_ref):
    mc = place[2]
    for h in range(keep_ref.shape[0]):
        s = slice(h * DH, (h + 1) * DH)
        keep_ref[h] = dot(left[mc, :, s], right[mc, :, s], 0, 0)
        send_ref[h] = dot(left[1 - mc, :, s], right[1 - mc, :, s], 0, 0).astype(BF16)


def state_body(place, k_ref, v_ref, q_hbm, keep_ref, send_ref, k_out, v_out, q_out, sem):
    copy = pltpu.make_async_copy(q_hbm, q_out, sem)
    copy.start()
    local_states(place, k_ref, v_ref, keep_ref, send_ref)
    k_out[...] = k_ref[...]
    v_out[...] = v_ref[...]
    copy.wait()


def chip_body(keep_ref, got_ref, out_ref):
    out_ref[...] = (keep_ref[...] + got_ref[...].astype(F32)).astype(BF16)


def first_axis_body(reverse, place, t_ref, g1, g2, g3, own_ref, m1, m2, m3):
    rows_first = place[2] == 0
    first = jnp.where(rows_first, place[1], place[0])
    second = jnp.where(rows_first, place[0], place[1])
    chip = t_ref[...].astype(F32)
    every, some = chip, jnp.zeros_like(chip)
    for d, g in ((1, g1), (2, g2), (3, g3)):
        value = g[...].astype(F32)
        every = every + value
        taken = first < d if reverse else first >= d
        some = some + jnp.where(taken, value, 0.0)
    own_ref[...] = some
    base = jnp.where(rows_first, 0.0, some)
    extra = jnp.where(rows_first, every, chip)
    for d, m in ((1, m1), (2, m2), (3, m3)):
        given = second + d >= 4 if reverse else second + d < 4
        m[...] = (base + jnp.where(given, extra, 0.0)).astype(BF16)


def second_axis_body(reverse, place, own_ref, g1, g2, g3, keep_ref, got_ref, out_ref, send_ref):
    total = own_ref[...]
    for g in (g1, g2, g3):
        total = total + g[...].astype(F32)
    late = place[2] == (0 if reverse else 1)
    out_ref[...] = (total + jnp.where(late, got_ref[...].astype(F32), 0.0)).astype(BF16)
    send_ref[...] = (total + jnp.where(late, 0.0, keep_ref[...])).astype(BF16)


def pick_state(place, own_ref, other_ref, b, h):
    return jnp.where(place[2] == b, own_ref[h], other_ref[h])


def each_batch(width, step):
    def body(b, carry):
        for h in range(width // DH):
            step(b, h, b * (width // DH) + h, slice(h * DH, (h + 1) * DH))
        return carry

    lax.fori_loop(0, 2, body, 0)


def masked_scores(lower, left, right):
    return jnp.where(lower, dot(left, right, 1, 1) * SCALE, 0.0).astype(BF16)


def intra_body(q_ref, k_ref, v_ref, intra_ref):
    lower = lower_mask(q_ref.shape[1])

    def step(b, h, i, s):
        scores = masked_scores(lower, q_ref[b, :, s], k_ref[b, :, s])
        intra_ref[b, :, s] = dot(scores, v_ref[b, :, s], 1, 0)

    each_batch(q_ref.shape[2], step)


def forward_body(place, q_ref, intra_ref, so_ref, sr_ref, normed_ref, attended_ref):
    def step(b, h, i, s):
        state = pick_state(place, so_ref, sr_ref, b, h)
        attended = intra_ref[b, :, s] + SCALE * dot(q_ref[b, :, s], state, 1, 0)
        attended_ref[b, :, s] = attended
        mean = jnp.mean(attended * attended, axis=-1, keepdims=True)
        normed_ref[b, :, s] = (attended / jnp.sqrt(mean + EPS)).astype(BF16)

    each_batch(q_ref.shape[2], step)


def project_body(n_ref, w_ref, out_hbm, buf, sem):
    chunks, _, width = buf.shape

    def out(j):
        return pltpu.make_async_copy(buf.at[j], out_hbm.at[j], sem.at[j])

    def body(i, carry):
        for j in (2 * i, 2 * i + 1):
            cols = pl.ds(pl.multiple_of(j * width, width), width)
            buf[j] = dot(n_ref[...], w_ref[:, cols], 1, 0).astype(BF16)
            out(j).start()
        return carry

    lax.fori_loop(0, chunks // 2, body, 0)
    for j in range(chunks):
        out(j).wait()


def half_body(first, x_ref, out_ref):
    out_ref[...] = x_ref[:, first : first + out_ref.shape[1]]


def combine_body(place, o_ref, g1, g2, g3, own_ref, s1, s2, s3):
    me = jnp.where(place[2] == 0, place[0], place[1])
    for d, out in enumerate((own_ref, s1, s2, s3)):
        i = (me + d) % 4
        total = o_ref[i].astype(F32)
        for g in (g1, g2, g3):
            total = total + g[i].astype(F32)
        out[...] = total.astype(out.dtype)


def finish_body(factor, own_ref, g1, g2, g3, out_ref):
    total = own_ref[...]
    for g in (g1, g2, g3):
        total = total + g[...].astype(F32)
    out_ref[...] = total * factor


def owner_of(place, step):
    return (place[3] + step + 8) % 8


def block_dot(place, step, ref, w_ref, first=0):
    width = w_ref.shape[0]
    start = pl.multiple_of(owner_of(place, step) * width + first, DH)
    return dot(ref[...], w_ref[:, pl.ds(start, ref.shape[1])], 1, 1)


def grad_near_body(steps, place, *refs):
    *blocks, w_ref, out_ref = refs
    total = block_dot(place, steps[0], blocks[0], w_ref)
    for step, ref in zip(steps[1:], blocks[1:]):
        total = total + block_dot(place, step, ref, w_ref)
    out_ref[...] = total


def grad_far_body(place, *refs):
    r4, l4, w_ref, sum_ref, a_ref, q_ref, ag_ref, keep_ref, send_ref, acc = refs
    _, width = sum_ref.shape
    half = block_dot(place, 4, r4, w_ref) + block_dot(place, 4, l4, w_ref, width // 2)
    acc[...] = (sum_ref[...] + half).reshape(acc.shape)

    def step(b, h, i, s):
        a, g = a_ref[b, :, s], acc[b, :, s]
        root = 1.0 / jnp.sqrt(jnp.mean(a * a, axis=-1, keepdims=True) + EPS)
        inner = jnp.mean(g * a, axis=-1, keepdims=True)
        ag_ref[b, :, s] = (g * root - a * (inner * root * root * root)).astype(BF16)

    each_batch(width, step)
    local_states(place, q_ref, ag_ref, keep_ref, send_ref)


def weight_tiles(place, mc, step):
    mx, my = place[0], place[1]
    k = owner_of(place, step)
    x = k // 2
    for j in range(2):
        y = 2 * (k % 2) + j
        far = jnp.where(mc == 0, (y - my + 4) % 4, (x - mx + 4) % 4)
        yield far, jnp.where(mc == 0, x, y)


def weight_pair(mc, n_ref, left, right, left_at, right_at):
    low = pl.multiple_of(mc * DH + left_at, DH)
    high = pl.multiple_of(mc * DH + right_at, DH)
    both = jnp.concatenate([left[:, pl.ds(low, DH)], right[:, pl.ds(high, DH)]], axis=1)
    r = dot(n_ref[...], both, 0, 0)
    return r[:, :DH], r[:, DH:]


def weight_near_body(steps, place, n_ref, *refs):
    *blocks, out_ref = refs
    mc = 1 - place[2]
    for step, ref in zip(steps, blocks):
        pieces = weight_pair(mc, n_ref, ref, ref, 0, 2 * DH)
        for (far, other), piece in zip(weight_tiles(place, mc, step), pieces):
            out_ref[far, other] = piece.astype(BF16)
    for far, other in weight_tiles(place, mc, 4):
        out_ref[far, other] = jnp.zeros(out_ref.shape[2:], BF16)


def weight_far_body(place, n_ref, r4, l4, out_ref):
    for j, piece in enumerate(weight_pair(1 - place[2], n_ref, r4, l4, 0, 0)):
        out_ref[j] = piece.astype(BF16)


def weight_add_body(steps, place, n_ref, *refs):
    *blocks, r4, l4, near_ref, far_ref, o0, o1, o2, o3, buf, sem = refs
    mc = place[2]
    for step, ref in zip(steps, blocks):
        pieces = weight_pair(mc, n_ref, ref, ref, 0, 2 * DH)
        for (far, other), piece in zip(weight_tiles(place, mc, step), pieces):
            buf[far, other] = (piece + near_ref[far, other].astype(F32)).astype(BF16)
    pieces = weight_pair(mc, n_ref, r4, l4, 0, 0)
    for j, ((far, other), piece) in enumerate(zip(weight_tiles(place, mc, 4), pieces)):
        buf[far, other] = (piece + far_ref[j].astype(F32)).astype(BF16)
    copies = [
        pltpu.make_async_copy(buf.at[d], o, sem.at[d]) for d, o in enumerate((o0, o1, o2, o3))
    ]
    for copy in copies:
        copy.start()
    for copy in copies:
        copy.wait()


def inner_body(place, q_ref, k_ref, v_ref, ag_ref, so, sr, dq_ref, dk_ref, dv_ref):
    lower = lower_mask(q_ref.shape[1])

    def step(b, h, i, s):
        ag = ag_ref[b, :, s]
        sg = masked_scores(lower, ag, v_ref[b, :, s])
        scores = masked_scores(lower, q_ref[b, :, s], k_ref[b, :, s])
        earlier = pick_state(place, so, sr, b, h)
        dq_ref[b, :, s] = (dot(sg, k_ref[b, :, s], 1, 0) + SCALE * dot(ag, earlier, 1, 1)).astype(BF16)
        dk_ref[b, :, s] = dot(sg, q_ref[b, :, s], 0, 0)
        dv_ref[b, :, s] = dot(scores, ag, 0, 0)

    each_batch(q_ref.shape[2], step)


def outer_body(place, k_ref, v_ref, ik_ref, iv_ref, go, gr, dk_ref, dv_ref):
    def step(b, h, i, s):
        later = pick_state(place, go, gr, b, h)
        dk_ref[b, :, s] = (ik_ref[b, :, s] + SCALE * dot(v_ref[b, :, s], later, 1, 1)).astype(BF16)
        dv_ref[b, :, s] = (iv_ref[b, :, s] + SCALE * dot(k_ref[b, :, s], later, 1, 0)).astype(BF16)

    each_batch(k_ref.shape[2], step)


def shift(value, axis, step):
    n = lax.axis_size(axis)
    return lax.ppermute(value, axis, [(i, (i + step) % n) for i in range(n)])


def shift_by_core(value, first, step):
    def target(x, y, c):
        along_y = (c == 0) == first
        return (x, (y + step) % 4, c) if along_y else ((x + step) % 4, y, c)

    def index(x, y, c):
        return (x * 4 + y) * 2 + c

    places = [(x, y, c) for x in range(4) for y in range(4) for c in range(2)]
    return lax.ppermute(value, CTX, [(index(*p), index(*target(*p))) for p in places])


def exclusive(place, keep, send, reverse):
    half, size = keep.shape, keep.size
    got = shift(send, "ctx_2", 1)
    chip = call(chip_body, [shape(half, BF16)], [keep, got], size)[0]
    near = []
    for d in (1, 2, 3):
        near.append(shift_by_core(chip, True, d))
    own, *out = call(
        functools.partial(first_axis_body, reverse),
        [shape(half, F32)] + [shape(half, BF16)] * 3,
        [place, chip, *near],
        size * 10,
        True,
    )
    far = []
    for d in (1, 2, 3):
        far.append(shift_by_core(out[d - 1], False, d))
    mine, other = call(
        functools.partial(second_axis_body, reverse),
        [shape(half, BF16)] * 2,
        [place, own, *far, keep, got],
        size * 8,
        True,
    )
    return mine, shift(other, "ctx_2", 1)


def gather_ring(block):
    near, right, left = [block], block, block
    rows, width = block.shape
    for i in (1, 2, 3, 4):
        if i == 4:
            half = [shape((rows, width // 2), BF16)]
            right = call(functools.partial(half_body, 0), half, [right], 0)[0]
            left = call(functools.partial(half_body, width // 2), half, [left], 0)[0]
        right = shift(right, "head", 1)
        left = shift(left, "head", -1)
        near += [right, left]
    return near


def send_near(place, normed, blocks):
    rows, width = normed.shape
    near = call(
        functools.partial(weight_near_body, STEPS),
        [shape((4, 4, width, DH), BF16)],
        [place, normed, *blocks[:7]],
        rows * width * width * 7,
        True,
    )[0]
    return shift(near, "ctx_2", 1)


def reduce_weight(place, normed, blocks, near, factor):
    rows, width = normed.shape
    flops = rows * width * width
    far = call(
        weight_far_body, [shape((2, width, DH), BF16)], [place, normed, *blocks[7:]], flops, True
    )[0]
    far = shift(far, "ctx_2", 1)
    whole = (4, width, DH)
    own, *send = call(
        functools.partial(weight_add_body, STEPS),
        [shape(whole, BF16)] * 4,
        [place, normed, *blocks, near, far],
        flops * 8,
        True,
        [VMEM((4, *whole), BF16), pltpu.SemaphoreType.DMA((4,))],
    )
    got = []
    for d in (1, 2, 3):
        got.append(shift_by_core(send[d - 1], True, d))
    piece = (width, DH)
    own, *send = call(
        combine_body,
        [shape(piece, F32)] + [shape(piece, BF16)] * 3,
        [place, own, *got],
        own.size * 4,
        True,
    )
    got = []
    for d in (1, 2, 3):
        got.append(shift_by_core(send[d - 1], False, d))
    return call(functools.partial(finish_body, factor), [shape(piece, F32)], [own, *got], own.size * 4)[0]


def layer(queries, key_rows, value_rows, out_weight, cotangent):
    _, length, width = queries.shape
    n_head = lax.axis_size("head")
    rows = 2 * length
    n_mat = 2 * width // DH
    half = (n_mat // 2, DH, DH)
    blocks = gather_ring(cotangent.reshape(rows, width))
    mx, my, mc, mz = (lax.axis_index(a) for a in (*CTX, "head"))
    place = jnp.stack([mx, my, mc, mz]).astype(jnp.int32)
    mat_flops = 2 * n_mat * length * DH * DH
    pair = [shape(half, F32), shape(half, BF16)]
    keep, send, near_keys, near_values, near_queries = call(
        state_body,
        pair + [shape(queries.shape, BF16)] * 3,
        [place, key_rows, value_rows, queries],
        mat_flops,
        True,
        [pltpu.SemaphoreType.DMA],
        pltpu.HBM,
    )
    intra = call(
        intra_body,
        [shape(queries.shape, F32)],
        [near_queries, near_keys, near_values],
        3 * mat_flops,
    )[0]
    state = exclusive(place, keep, send, False)
    normed, attended = call(
        forward_body,
        [shape(queries.shape, BF16), shape(queries.shape, F32)],
        [place, near_queries, intra, *state],
        mat_flops,
        True,
    )
    normed = normed.reshape(rows, width)
    big = 2 * rows * width * width * n_head
    partial = call(
        project_body,
        [shape((n_head, rows, width), BF16)],
        [normed, out_weight],
        big,
        scratch=[VMEM((n_head, rows, width), BF16), pltpu.SemaphoreType.DMA((n_head,))],
        result=pltpu.HBM,
    )[0]
    layer_output = lax.psum_scatter(
        partial.reshape(n_head * rows, width), "head", scatter_dimension=0, tiled=True
    ).reshape(queries.shape)
    near = send_near(place, normed, blocks)
    part_grad = call(
        functools.partial(grad_near_body, STEPS),
        [shape((rows, width), F32)],
        [place, *blocks[:7], out_weight],
        big * 7 // 8,
        True,
    )[0]
    attended_grad, keep, send = call(
        grad_far_body,
        [shape(queries.shape, BF16), *pair],
        [place, *blocks[7:], out_weight, part_grad, attended, queries],
        big // 8,
        True,
        [VMEM(queries.shape, F32)],
    )
    factor = (rows * lax.axis_size(CTX)) ** (-0.5)
    weight_grad = reduce_weight(place, normed, blocks, near, factor)
    grad_state = exclusive(place, keep, send, True)
    query_grad, inner_key, inner_value = call(
        inner_body,
        [shape(queries.shape, BF16)] + [shape(queries.shape, F32)] * 2,
        [place, queries, key_rows, value_rows, attended_grad, *state],
        5 * mat_flops,
        True,
    )
    key_grad, value_grad = call(
        outer_body,
        [shape(queries.shape, BF16)] * 2,
        [place, key_rows, value_rows, inner_key, inner_value, *grad_state],
        2 * mat_flops,
        True,
    )
    return (layer_output, query_grad, key_grad, value_grad, weight_grad)


def solution(mesh):
    split = Mesh(
        mesh.devices.reshape(4, 4, 2, mesh.shape["head"]), ("ctx_0", "ctx_1", "ctx_2", "head")
    )
    rows = P(None, CTX, "head")
    return jax.shard_map(
        layer,
        mesh=split,
        in_specs=(rows, rows, rows, P("head", None), rows),
        out_specs=(rows, rows, rows, rows, P("head", CTX)),
        check_vma=False,
    )
```

```python
import functools

import jax
import jax.numpy as jnp
from jax import lax
from jax.experimental import pallas as pl
from jax.experimental.pallas import tpu as pltpu
from jax.sharding import Mesh
from jax.sharding import PartitionSpec as P

DH = 128
CTX = ("ctx_0", "ctx_1", "ctx_2")
SCALE = DH ** (-0.5)
EPS = 1e-06
F32, BF16 = jnp.float32, jnp.bfloat16
VMEM = pltpu.VMEM
LIMIT = 20 << 20
SMEM = pltpu.SMEM
STEPS = (0, -1, 1, -2, 2, -3, 3)


def dot(a, b, ca, cb):
    return lax.dot_general(a, b, (((ca,), (cb,)), ((), ())), preferred_element_type=F32)


def call(body, outs, args, flops, scalar=False, scratch=(), last=VMEM):
    size = sum(a.size * a.dtype.itemsize for a in args)
    size += sum(o.size * o.dtype.itemsize for o in outs)
    cost = pl.CostEstimate(flops=flops, bytes_accessed=size, transcendentals=0)
    specs = [pl.BlockSpec(memory_space=VMEM)] * len(args)
    specs[-1] = pl.BlockSpec(memory_space=last)
    if scalar:
        specs[0] = pl.BlockSpec(memory_space=SMEM)
    return pl.pallas_call(
        body,
        out_shape=outs,
        in_specs=specs,
        out_specs=[pl.BlockSpec(memory_space=VMEM)] * len(outs),
        scratch_shapes=list(scratch),
        cost_estimate=cost,
        compiler_params=pltpu.CompilerParams(vmem_limit_bytes=LIMIT),
    )(*args)


def shape(dims, dtype):
    return jax.ShapeDtypeStruct(dims, dtype)


def lower_mask(n):
    return lax.broadcasted_iota(jnp.int32, (n, n), 0) >= lax.broadcasted_iota(jnp.int32, (n, n), 1)


def local_states(place, left, right, keep_ref, send_ref):
    mc = place[2]

    def body(h, carry):
        s = pl.ds(pl.multiple_of(h * DH, DH), DH)
        keep_ref[h] = dot(left[mc, :, s], right[mc, :, s], 0, 0)
        send_ref[h] = dot(left[1 - mc, :, s], right[1 - mc, :, s], 0, 0).astype(BF16)
        return carry

    lax.fori_loop(0, keep_ref.shape[0], body, 0)


def state_body(place, k_ref, v_ref, q_hbm, keep_ref, send_ref, k_out, v_out, q_out, sem):
    copy = pltpu.make_async_copy(q_hbm, q_out, sem)
    copy.start()
    local_states(place, k_ref, v_ref, keep_ref, send_ref)
    k_out[...] = k_ref[...]
    v_out[...] = v_ref[...]
    copy.wait()


def chip_body(keep_ref, got_ref, out_ref):
    out_ref[...] = (keep_ref[...] + got_ref[...].astype(F32)).astype(BF16)


def first_axis_body(reverse, place, t_ref, g1, g2, g3, own_ref, m1, m2, m3):
    rows_first = place[2] == 0
    first = jnp.where(rows_first, place[1], place[0])
    second = jnp.where(rows_first, place[0], place[1])

    def body(h, carry):
        chip = t_ref[h].astype(F32)
        every, some = chip, jnp.zeros_like(chip)
        for d, g in ((1, g1), (2, g2), (3, g3)):
            value = g[h].astype(F32)
            every = every + value
            taken = first < d if reverse else first >= d
            some = some + jnp.where(taken, value, 0.0)
        own_ref[h] = some
        base = jnp.where(rows_first, 0.0, some)
        extra = jnp.where(rows_first, every, chip)
        for d, m in ((1, m1), (2, m2), (3, m3)):
            given = second + d >= 4 if reverse else second + d < 4
            m[h] = (base + jnp.where(given, extra, 0.0)).astype(BF16)
        return carry

    lax.fori_loop(0, t_ref.shape[0], body, 0)


def second_axis_body(reverse, place, own_ref, g1, g2, g3, keep_ref, got_ref, out_ref, send_ref):
    total = own_ref[...]
    for g in (g1, g2, g3):
        total = total + g[...].astype(F32)
    late = place[2] == (0 if reverse else 1)
    out_ref[...] = (total + jnp.where(late, got_ref[...].astype(F32), 0.0)).astype(BF16)
    send_ref[...] = (total + jnp.where(late, 0.0, keep_ref[...])).astype(BF16)


def pick_state(place, own_ref, other_ref, b, h):
    return jnp.where(place[2] == b, own_ref[h], other_ref[h])


def each_head(width, step, group=2):
    n = width // DH

    def body(i, carry):
        for j in range(group):
            b, h = i // (n // group), group * (i % (n // group)) + j
            step(b, h, b * n + h, pl.ds(pl.multiple_of(h * DH, DH), DH))
        return carry

    lax.fori_loop(0, 2 * n // group, body, 0)


def masked_scores(lower, left, right):
    return jnp.where(lower, dot(left, right, 1, 1) * SCALE, 0.0).astype(BF16)


def intra_body(q_ref, k_ref, v_ref, intra_ref):
    lower = lower_mask(q_ref.shape[1])

    def step(b, h, i, s):
        scores = masked_scores(lower, q_ref[b, :, s], k_ref[b, :, s])
        intra_ref[b, :, s] = dot(scores, v_ref[b, :, s], 1, 0)

    each_head(q_ref.shape[2], step)


def forward_body(place, q_ref, intra_ref, so_ref, sr_ref, normed_ref, attended_ref):
    def step(b, h, i, s):
        state = pick_state(place, so_ref, sr_ref, b, h)
        attended = intra_ref[b, :, s] + SCALE * dot(q_ref[b, :, s], state, 1, 0)
        attended_ref[b, :, s] = attended
        mean = jnp.mean(attended * attended, axis=-1, keepdims=True)
        normed_ref[b, :, s] = (attended / jnp.sqrt(mean + EPS)).astype(BF16)

    each_head(q_ref.shape[2], step)


def half_body(first, x_ref, out_ref):
    out_ref[...] = x_ref[:, first : first + out_ref.shape[1]]


def combine_body(place, o_ref, g1, g2, g3, own_ref, s1, s2, s3):
    me = jnp.where(place[2] == 0, place[0], place[1])
    step = 128

    def body(k, carry):
        part = pl.ds(pl.multiple_of(k * step, step), step)
        for d, out in enumerate((own_ref, s1, s2, s3)):
            i = (me + d) % 4
            total = o_ref[i, part].astype(F32)
            for g in (g1, g2, g3):
                total = total + g[i, part].astype(F32)
            out[part] = total.astype(out.dtype)
        return carry

    lax.fori_loop(0, own_ref.shape[0] // step, body, 0)


def finish_body(factor, own_ref, g1, g2, g3, out_ref):
    total = own_ref[...]
    for g in (g1, g2, g3):
        total = total + g[...].astype(F32)
    out_ref[...] = total * factor


def owner_of(place, step):
    return (place[3] + step + 8) % 8


def block_dot(place, step, ref, w_ref, first=0):
    width = w_ref.shape[0]
    start = pl.multiple_of(owner_of(place, step) * width + first, DH)
    return dot(ref[...], w_ref[:, pl.ds(start, ref.shape[1])], 1, 1)


def column_product(place, step, n_ref, w_ref):
    width = n_ref.shape[1]
    start = pl.multiple_of(owner_of(place, step) * width, width)
    return dot(n_ref[...], w_ref[:, pl.ds(start, width)], 1, 0)


def out_first_body(place, n_ref, w_ref, right_ref, left_ref):
    half = right_ref.shape[1]
    total = column_product(place, 4, n_ref, w_ref)
    right_ref[...] = total[:, :half].astype(BF16)
    left_ref[...] = total[:, half:].astype(BF16)


def out_step_body(step, place, n_ref, w_ref, r_ref, l_ref, right_ref, left_ref):
    half = n_ref.shape[1] // 2
    right = column_product(place, step, n_ref, w_ref)
    left = column_product(place, -step, n_ref, w_ref)
    if step == 3:
        right_ref[:, :half] = (right[:, :half] + r_ref[...].astype(F32)).astype(BF16)
        right_ref[:, half:] = right[:, half:].astype(BF16)
        left_ref[:, :half] = left[:, :half].astype(BF16)
        left_ref[:, half:] = (left[:, half:] + l_ref[...].astype(F32)).astype(BF16)
    else:
        right_ref[...] = (right + r_ref[...].astype(F32)).astype(BF16)
        left_ref[...] = (left + l_ref[...].astype(F32)).astype(BF16)


def out_last_body(place, n_ref, w_ref, r_ref, l_ref, out_ref):
    total = column_product(place, 0, n_ref, w_ref)
    out_ref[...] = (total + r_ref[...].astype(F32) + l_ref[...].astype(F32)).astype(BF16)


def grad_near_body(steps, place, *refs):
    *blocks, w_ref, out_ref = refs
    total = block_dot(place, steps[0], blocks[0], w_ref)
    for step, ref in zip(steps[1:], blocks[1:]):
        total = total + block_dot(place, step, ref, w_ref)
    out_ref[...] = total


def grad_far_body(place, *refs):
    r4, l4, w_ref, sum_ref, a_ref, q_ref, ag_ref, keep_ref, send_ref, acc = refs
    _, width = sum_ref.shape
    half = block_dot(place, 4, r4, w_ref) + block_dot(place, 4, l4, w_ref, width // 2)
    acc[...] = (sum_ref[...] + half).reshape(acc.shape)

    def step(b, h, i, s):
        a, g = a_ref[b, :, s], acc[b, :, s]
        root = 1.0 / jnp.sqrt(jnp.mean(a * a, axis=-1, keepdims=True) + EPS)
        inner = jnp.mean(g * a, axis=-1, keepdims=True)
        ag_ref[b, :, s] = (g * root - a * (inner * root * root * root)).astype(BF16)

    each_head(width, step, 1)
    local_states(place, q_ref, ag_ref, keep_ref, send_ref)


def weight_tiles(place, mc, step):
    mx, my = place[0], place[1]
    k = owner_of(place, step)
    x = k // 2
    for j in range(2):
        y = 2 * (k % 2) + j
        far = jnp.where(mc == 0, (y - my + 4) % 4, (x - mx + 4) % 4)
        yield far, jnp.where(mc == 0, x, y)


def weight_pair(mc, n_ref, left, right, left_at, right_at):
    low = pl.multiple_of(mc * DH + left_at, DH)
    high = pl.multiple_of(mc * DH + right_at, DH)
    both = jnp.concatenate([left[:, pl.ds(low, DH)], right[:, pl.ds(high, DH)]], axis=1)
    r = dot(n_ref[...], both, 0, 0)
    return r[:, :DH], r[:, DH:]


def weight_near_body(steps, place, n_ref, *refs):
    *blocks, out_ref = refs
    mc = 1 - place[2]
    for step, ref in zip(steps, blocks):
        pieces = weight_pair(mc, n_ref, ref, ref, 0, 2 * DH)
        for (far, other), piece in zip(weight_tiles(place, mc, step), pieces):
            out_ref[far, other] = piece.astype(BF16)
    for far, other in weight_tiles(place, mc, 4):
        out_ref[far, other] = jnp.zeros(out_ref.shape[2:], BF16)


def weight_far_body(place, n_ref, r4, l4, out_ref):
    for j, piece in enumerate(weight_pair(1 - place[2], n_ref, r4, l4, 0, 0)):
        out_ref[j] = piece.astype(BF16)


def weight_add_body(steps, place, n_ref, *refs):
    *blocks, r4, l4, near_ref, far_ref, o0, o1, o2, o3, buf, sem = refs
    mc = place[2]
    for step, ref in zip(steps, blocks):
        pieces = weight_pair(mc, n_ref, ref, ref, 0, 2 * DH)
        for (far, other), piece in zip(weight_tiles(place, mc, step), pieces):
            buf[far, other] = (piece + near_ref[far, other].astype(F32)).astype(BF16)
    pieces = weight_pair(mc, n_ref, r4, l4, 0, 0)
    for j, ((far, other), piece) in enumerate(zip(weight_tiles(place, mc, 4), pieces)):
        buf[far, other] = (piece + far_ref[j].astype(F32)).astype(BF16)
    copies = [
        pltpu.make_async_copy(buf.at[d], o, sem.at[d]) for d, o in enumerate((o0, o1, o2, o3))
    ]
    for copy in copies:
        copy.start()
    for copy in copies:
        copy.wait()


def inner_body(place, q_ref, k_ref, v_ref, ag_ref, so, sr, dq_ref, dk_ref, dv_ref):
    lower = lower_mask(q_ref.shape[1])

    def step(b, h, i, s):
        ag = ag_ref[b, :, s]
        sg = masked_scores(lower, ag, v_ref[b, :, s])
        scores = masked_scores(lower, q_ref[b, :, s], k_ref[b, :, s])
        earlier = pick_state(place, so, sr, b, h)
        dq_ref[b, :, s] = (dot(sg, k_ref[b, :, s], 1, 0) + SCALE * dot(ag, earlier, 1, 1)).astype(BF16)
        dk_ref[b, :, s] = dot(sg, q_ref[b, :, s], 0, 0)
        dv_ref[b, :, s] = dot(scores, ag, 0, 0)

    each_head(q_ref.shape[2], step)


def outer_body(place, k_ref, v_ref, ik_ref, iv_ref, go, gr, dk_ref, dv_ref):
    def step(b, h, i, s):
        later = pick_state(place, go, gr, b, h)
        dk_ref[b, :, s] = (ik_ref[b, :, s] + SCALE * dot(v_ref[b, :, s], later, 1, 1)).astype(BF16)
        dv_ref[b, :, s] = (iv_ref[b, :, s] + SCALE * dot(k_ref[b, :, s], later, 1, 0)).astype(BF16)

    each_head(k_ref.shape[2], step, 1)


def shift(value, axis, step):
    n = lax.axis_size(axis)
    return lax.ppermute(value, axis, [(i, (i + step) % n) for i in range(n)])


def shift_by_core(value, first, step):
    def target(x, y, c):
        along_y = (c == 0) == first
        return (x, (y + step) % 4, c) if along_y else ((x + step) % 4, y, c)

    def index(x, y, c):
        return (x * 4 + y) * 2 + c

    places = [(x, y, c) for x in range(4) for y in range(4) for c in range(2)]
    return lax.ppermute(value, CTX, [(index(*p), index(*target(*p))) for p in places])


def exclusive(place, keep, send, reverse):
    half, size = keep.shape, keep.size
    got = shift(send, "ctx_2", 1)
    chip = call(chip_body, [shape(half, BF16)], [keep, got], size)[0]
    near = []
    for d in (1, 2, 3):
        near.append(shift_by_core(chip, True, d))
    own, *out = call(
        functools.partial(first_axis_body, reverse),
        [shape(half, F32)] + [shape(half, BF16)] * 3,
        [place, chip, *near],
        size * 10,
        True,
    )
    far = []
    for d in (1, 2, 3):
        far.append(shift_by_core(out[d - 1], False, d))
    mine, other = call(
        functools.partial(second_axis_body, reverse),
        [shape(half, BF16)] * 2,
        [place, own, *far, keep, got],
        size * 8,
        True,
    )
    return mine, shift(other, "ctx_2", 1)


def gather_ring(block):
    near, right, left = [block], block, block
    rows, width = block.shape
    for i in (1, 2, 3, 4):
        if i == 4:
            half = [shape((rows, width // 2), BF16)]
            right = call(functools.partial(half_body, 0), half, [right], 0)[0]
            left = call(functools.partial(half_body, width // 2), half, [left], 0)[0]
        right = shift(right, "head", 1)
        left = shift(left, "head", -1)
        near += [right, left]
    return near


def output_ring(place, normed, weight):
    rows, width = normed.shape
    flops = 2 * rows * width * width
    half, whole = [shape((rows, width // 2), BF16)] * 2, [shape((rows, width), BF16)] * 2
    right, left = call(out_first_body, half, [place, normed, weight], flops, True)
    for step in (3, 2, 1):
        right = shift(right, "head", 1)
        left = shift(left, "head", -1)
        right, left = call(
            functools.partial(out_step_body, step),
            whole,
            [place, normed, weight, right, left],
            2 * flops,
            True,
        )
    right = shift(right, "head", 1)
    left = shift(left, "head", -1)
    return call(out_last_body, whole[:1], [place, normed, weight, right, left], flops, True)[0]


def send_near(place, normed, blocks):
    rows, width = normed.shape
    near = call(
        functools.partial(weight_near_body, STEPS),
        [shape((4, 4, width, DH), BF16)],
        [place, normed, *blocks[:7]],
        rows * width * width * 7,
        True,
    )[0]
    return shift(near, "ctx_2", 1)


def reduce_weight(place, normed, blocks, near, factor):
    rows, width = normed.shape
    flops = rows * width * width
    far = call(
        weight_far_body, [shape((2, width, DH), BF16)], [place, normed, *blocks[7:]], flops, True
    )[0]
    far = shift(far, "ctx_2", 1)
    whole = (4, width, DH)
    own, *send = call(
        functools.partial(weight_add_body, STEPS),
        [shape(whole, BF16)] * 4,
        [place, normed, *blocks, near, far],
        flops * 8,
        True,
        [VMEM((4, *whole), BF16), pltpu.SemaphoreType.DMA((4,))],
    )
    got = []
    for d in (1, 2, 3):
        got.append(shift_by_core(send[d - 1], True, d))
    piece = (width, DH)
    own, *send = call(
        combine_body,
        [shape(piece, F32)] + [shape(piece, BF16)] * 3,
        [place, own, *got],
        own.size * 4,
        True,
    )
    got = []
    for d in (1, 2, 3):
        got.append(shift_by_core(send[d - 1], False, d))
    return call(functools.partial(finish_body, factor), [shape(piece, F32)], [own, *got], own.size * 4)[0]


def layer(queries, key_rows, value_rows, out_weight, cotangent):
    _, length, width = queries.shape
    n_head = lax.axis_size("head")
    rows = 2 * length
    n_mat = 2 * width // DH
    half = (n_mat // 2, DH, DH)
    blocks = gather_ring(cotangent.reshape(rows, width))
    mx, my, mc, mz = (lax.axis_index(a) for a in (*CTX, "head"))
    place = jnp.stack([mx, my, mc, mz]).astype(jnp.int32)
    mat_flops = 2 * n_mat * length * DH * DH
    pair = [shape(half, F32), shape(half, BF16)]
    keep, send, near_keys, near_values, near_queries = call(
        state_body,
        pair + [shape(queries.shape, BF16)] * 3,
        [place, key_rows, value_rows, queries],
        mat_flops,
        True,
        [pltpu.SemaphoreType.DMA],
        pltpu.HBM,
    )
    intra = call(
        intra_body,
        [shape(queries.shape, F32)],
        [near_queries, near_keys, near_values],
        3 * mat_flops,
    )[0]
    state = exclusive(place, keep, send, False)
    normed, attended = call(
        forward_body,
        [shape(queries.shape, BF16), shape(queries.shape, F32)],
        [place, near_queries, intra, *state],
        mat_flops,
        True,
    )
    normed = normed.reshape(rows, width)
    big = 2 * rows * width * width * n_head
    layer_output = output_ring(place, normed, out_weight).reshape(queries.shape)
    near = send_near(place, normed, blocks)
    part_grad = call(
        functools.partial(grad_near_body, STEPS),
        [shape((rows, width), F32)],
        [place, *blocks[:7], out_weight],
        big * 7 // 8,
        True,
    )[0]
    attended_grad, keep, send = call(
        grad_far_body,
        [shape(queries.shape, BF16), *pair],
        [place, *blocks[7:], out_weight, part_grad, attended, queries],
        big // 8,
        True,
        [VMEM(queries.shape, F32)],
    )
    factor = (rows * lax.axis_size(CTX)) ** (-0.5)
    weight_grad = reduce_weight(place, normed, blocks, near, factor)
    grad_state = exclusive(place, keep, send, True)
    query_grad, inner_key, inner_value = call(
        inner_body,
        [shape(queries.shape, BF16)] + [shape(queries.shape, F32)] * 2,
        [place, queries, key_rows, value_rows, attended_grad, *state],
        5 * mat_flops,
        True,
    )
    key_grad, value_grad = call(
        outer_body,
        [shape(queries.shape, BF16)] * 2,
        [place, key_rows, value_rows, inner_key, inner_value, *grad_state],
        2 * mat_flops,
        True,
    )
    return (layer_output, query_grad, key_grad, value_grad, weight_grad)


def solution(mesh):
    split = Mesh(
        mesh.devices.reshape(4, 4, 2, mesh.shape["head"]), ("ctx_0", "ctx_1", "ctx_2", "head")
    )
    rows = P(None, CTX, "head")
    return jax.shard_map(
        layer,
        mesh=split,
        in_specs=(rows, rows, rows, P("head", None), rows),
        out_specs=(rows, rows, rows, rows, P("head", CTX)),
        check_vma=False,
    )
```

```python
import functools

import jax
import jax.numpy as jnp
from jax import lax
from jax.experimental import pallas as pl
from jax.experimental.pallas import tpu as pltpu
from jax.sharding import Mesh
from jax.sharding import PartitionSpec as P

DH = 128
CTX = ("ctx_0", "ctx_1", "ctx_2")
SCALE = DH ** (-0.5)
EPS = 1e-06
F32, BF16 = jnp.float32, jnp.bfloat16
VMEM = pltpu.VMEM
LIMIT = 20 << 20
SMEM = pltpu.SMEM
STEPS = (0, -1, 1, -2, 2, -3, 3)


def dot(a, b, ca, cb):
    return lax.dot_general(a, b, (((ca,), (cb,)), ((), ())), preferred_element_type=F32)


def call(body, outs, args, flops, scalar=False, scratch=(), last=VMEM):
    size = sum(a.size * a.dtype.itemsize for a in args)
    size += sum(o.size * o.dtype.itemsize for o in outs)
    cost = pl.CostEstimate(flops=flops, bytes_accessed=size, transcendentals=0)
    specs = [pl.BlockSpec(memory_space=VMEM)] * len(args)
    specs[-1] = pl.BlockSpec(memory_space=last)
    if scalar:
        specs[0] = pl.BlockSpec(memory_space=SMEM)
    return pl.pallas_call(
        body,
        out_shape=outs,
        in_specs=specs,
        out_specs=[pl.BlockSpec(memory_space=VMEM)] * len(outs),
        scratch_shapes=list(scratch),
        cost_estimate=cost,
        compiler_params=pltpu.CompilerParams(vmem_limit_bytes=LIMIT),
    )(*args)


def shape(dims, dtype):
    return jax.ShapeDtypeStruct(dims, dtype)


def lower_mask(n):
    return lax.broadcasted_iota(jnp.int32, (n, n), 0) >= lax.broadcasted_iota(jnp.int32, (n, n), 1)


def local_states(place, left, right, keep_ref, send_ref):
    mc = place[2]

    def body(i, carry):
        for h in (2 * i, 2 * i + 1):
            s = pl.ds(pl.multiple_of(h * DH, DH), DH)
            keep_ref[h] = dot(left[mc, :, s], right[mc, :, s], 0, 0)
            send_ref[h] = dot(left[1 - mc, :, s], right[1 - mc, :, s], 0, 0).astype(BF16)
        return carry

    lax.fori_loop(0, keep_ref.shape[0] // 2, body, 0)


def state_body(place, k_ref, v_ref, q_hbm, keep_ref, send_ref, k_out, v_out, q_out, sem):
    copy = pltpu.make_async_copy(q_hbm, q_out, sem)
    copy.start()
    local_states(place, k_ref, v_ref, keep_ref, send_ref)
    k_out[...] = k_ref[...]
    v_out[...] = v_ref[...]
    copy.wait()


def chip_body(keep_ref, got_ref, out_ref):
    out_ref[...] = (keep_ref[...] + got_ref[...].astype(F32)).astype(BF16)


def first_axis_body(reverse, place, t_ref, g1, g2, g3, own_ref, m1, m2, m3):
    rows_first = place[2] == 0
    first = jnp.where(rows_first, place[1], place[0])
    second = jnp.where(rows_first, place[0], place[1])

    def body(h, carry):
        chip = t_ref[h].astype(F32)
        every, some = chip, jnp.zeros_like(chip)
        for d, g in ((1, g1), (2, g2), (3, g3)):
            value = g[h].astype(F32)
            every = every + value
            taken = first < d if reverse else first >= d
            some = some + jnp.where(taken, value, 0.0)
        own_ref[h] = some
        base = jnp.where(rows_first, 0.0, some)
        extra = jnp.where(rows_first, every, chip)
        for d, m in ((1, m1), (2, m2), (3, m3)):
            given = second + d >= 4 if reverse else second + d < 4
            m[h] = (base + jnp.where(given, extra, 0.0)).astype(BF16)
        return carry

    lax.fori_loop(0, t_ref.shape[0], body, 0)


def second_axis_body(reverse, place, own_ref, g1, g2, g3, keep_ref, got_ref, out_ref, send_ref):
    total = own_ref[...]
    for g in (g1, g2, g3):
        total = total + g[...].astype(F32)
    late = place[2] == (0 if reverse else 1)
    out_ref[...] = (total + jnp.where(late, got_ref[...].astype(F32), 0.0)).astype(BF16)
    send_ref[...] = (total + jnp.where(late, 0.0, keep_ref[...])).astype(BF16)


def pick_state(place, own_ref, other_ref, b, h):
    return jnp.where(place[2] == b, own_ref[h], other_ref[h])


def each_batch(width, step):
    def body(b, carry):
        for h in range(width // DH):
            step(b, h, b * (width // DH) + h, slice(h * DH, (h + 1) * DH))
        return carry

    lax.fori_loop(0, 2, body, 0)


def each_head(width, step, group=2):
    n = width // DH

    def body(i, carry):
        for j in range(group):
            b, h = i // (n // group), group * (i % (n // group)) + j
            step(b, h, b * n + h, pl.ds(pl.multiple_of(h * DH, DH), DH))
        return carry

    lax.fori_loop(0, 2 * n // group, body, 0)


def masked_scores(lower, left, right):
    return jnp.where(lower, dot(left, right, 1, 1) * SCALE, 0.0).astype(BF16)


def intra_body(q_ref, k_ref, v_ref, intra_ref):
    lower = lower_mask(q_ref.shape[1])

    def step(b, h, i, s):
        scores = masked_scores(lower, q_ref[b, :, s], k_ref[b, :, s])
        intra_ref[b, :, s] = dot(scores, v_ref[b, :, s], 1, 0)

    each_batch(q_ref.shape[2], step)


def forward_body(place, q_ref, intra_ref, so_ref, sr_ref, normed_ref, attended_ref):
    def step(b, h, i, s):
        state = pick_state(place, so_ref, sr_ref, b, h)
        attended = intra_ref[b, :, s] + SCALE * dot(q_ref[b, :, s], state, 1, 0)
        attended_ref[b, :, s] = attended
        mean = jnp.mean(attended * attended, axis=-1, keepdims=True)
        normed_ref[b, :, s] = (attended / jnp.sqrt(mean + EPS)).astype(BF16)

    each_batch(q_ref.shape[2], step)


def half_body(first, x_ref, out_ref):
    out_ref[...] = x_ref[:, first : first + out_ref.shape[1]]


def combine_body(place, o_ref, g1, g2, g3, own_ref, s1, s2, s3):
    me = jnp.where(place[2] == 0, place[0], place[1])
    step = 128

    def body(k, carry):
        part = pl.ds(pl.multiple_of(k * step, step), step)
        for d, out in enumerate((own_ref, s1, s2, s3)):
            i = (me + d) % 4
            total = o_ref[i, part].astype(F32)
            for g in (g1, g2, g3):
                total = total + g[i, part].astype(F32)
            out[part] = total.astype(out.dtype)
        return carry

    lax.fori_loop(0, own_ref.shape[0] // step, body, 0)


def finish_body(factor, own_ref, g1, g2, g3, out_ref):
    total = own_ref[...]
    for g in (g1, g2, g3):
        total = total + g[...].astype(F32)
    out_ref[...] = total * factor


def owner_of(place, step):
    return (place[3] + step + 8) % 8


def block_dot(place, step, ref, w_ref, first=0):
    width = w_ref.shape[0]
    start = pl.multiple_of(owner_of(place, step) * width + first, DH)
    return dot(ref[...], w_ref[:, pl.ds(start, ref.shape[1])], 1, 1)


def column_product(place, step, n_ref, w_ref):
    width = n_ref.shape[1]
    start = pl.multiple_of(owner_of(place, step) * width, width)
    return dot(n_ref[...], w_ref[:, pl.ds(start, width)], 1, 0)


def out_first_body(place, n_ref, w_ref, right_ref, left_ref):
    half = right_ref.shape[1]
    total = column_product(place, 4, n_ref, w_ref)
    right_ref[...] = total[:, :half].astype(BF16)
    left_ref[...] = total[:, half:].astype(BF16)


def out_step_body(step, place, n_ref, w_ref, r_ref, l_ref, right_ref, left_ref):
    half = n_ref.shape[1] // 2
    right = column_product(place, step, n_ref, w_ref)
    left = column_product(place, -step, n_ref, w_ref)
    if step == 3:
        right_ref[:, :half] = (right[:, :half] + r_ref[...].astype(F32)).astype(BF16)
        right_ref[:, half:] = right[:, half:].astype(BF16)
        left_ref[:, :half] = left[:, :half].astype(BF16)
        left_ref[:, half:] = (left[:, half:] + l_ref[...].astype(F32)).astype(BF16)
    else:
        right_ref[...] = (right + r_ref[...].astype(F32)).astype(BF16)
        left_ref[...] = (left + l_ref[...].astype(F32)).astype(BF16)


def out_last_body(place, n_ref, w_ref, r_ref, l_ref, out_ref):
    total = column_product(place, 0, n_ref, w_ref)
    out_ref[...] = (total + r_ref[...].astype(F32) + l_ref[...].astype(F32)).astype(BF16)


def grad_near_body(steps, place, *refs):
    *blocks, w_ref, out_ref = refs
    total = block_dot(place, steps[0], blocks[0], w_ref)
    for step, ref in zip(steps[1:], blocks[1:]):
        total = total + block_dot(place, step, ref, w_ref)
    out_ref[...] = total


def grad_far_body(place, *refs):
    r4, l4, w_ref, sum_ref, a_ref, q_ref, ag_ref, keep_ref, send_ref, acc = refs
    _, width = sum_ref.shape
    half = block_dot(place, 4, r4, w_ref) + block_dot(place, 4, l4, w_ref, width // 2)
    acc[...] = (sum_ref[...] + half).reshape(acc.shape)

    def step(b, h, i, s):
        a, g = a_ref[b, :, s], acc[b, :, s]
        root = 1.0 / jnp.sqrt(jnp.mean(a * a, axis=-1, keepdims=True) + EPS)
        inner = jnp.mean(g * a, axis=-1, keepdims=True)
        ag_ref[b, :, s] = (g * root - a * (inner * root * root * root)).astype(BF16)

    each_head(width, step, 2)
    local_states(place, q_ref, ag_ref, keep_ref, send_ref)


def weight_tiles(place, mc, step):
    mx, my = place[0], place[1]
    k = owner_of(place, step)
    x = k // 2
    for j in range(2):
        y = 2 * (k % 2) + j
        far = jnp.where(mc == 0, (y - my + 4) % 4, (x - mx + 4) % 4)
        yield far, jnp.where(mc == 0, x, y)


def weight_pair(mc, n_ref, left, right, left_at, right_at):
    low = pl.multiple_of(mc * DH + left_at, DH)
    high = pl.multiple_of(mc * DH + right_at, DH)
    both = jnp.concatenate([left[:, pl.ds(low, DH)], right[:, pl.ds(high, DH)]], axis=1)
    r = dot(n_ref[...], both, 0, 0)
    return r[:, :DH], r[:, DH:]


def weight_out_body(steps, place, n_ref, *refs):
    *blocks, r4, l4, out_ref = refs
    mc = 1 - place[2]
    for step, ref in zip(steps, blocks):
        pieces = weight_pair(mc, n_ref, ref, ref, 0, 2 * DH)
        for (far, other), piece in zip(weight_tiles(place, mc, step), pieces):
            out_ref[far, other] = piece.astype(BF16)
    pieces = weight_pair(mc, n_ref, r4, l4, 0, 0)
    for (far, other), piece in zip(weight_tiles(place, mc, 4), pieces):
        out_ref[far, other] = piece.astype(BF16)


def weight_add_body(steps, place, n_ref, *refs):
    *blocks, r4, l4, in_ref, o0, o1, o2, o3, buf, sem = refs
    mc = place[2]
    for step, ref in zip(steps, blocks):
        pieces = weight_pair(mc, n_ref, ref, ref, 0, 2 * DH)
        for (far, other), piece in zip(weight_tiles(place, mc, step), pieces):
            buf[far, other] = (piece + in_ref[far, other].astype(F32)).astype(BF16)
    pieces = weight_pair(mc, n_ref, r4, l4, 0, 0)
    for (far, other), piece in zip(weight_tiles(place, mc, 4), pieces):
        buf[far, other] = (piece + in_ref[far, other].astype(F32)).astype(BF16)
    copies = [
        pltpu.make_async_copy(buf.at[d], o, sem.at[d]) for d, o in enumerate((o0, o1, o2, o3))
    ]
    for copy in copies:
        copy.start()
    for copy in copies:
        copy.wait()


def inner_body(place, q_ref, k_ref, v_ref, ag_ref, so, sr, dq_ref, dk_ref, dv_ref):
    lower = lower_mask(q_ref.shape[1])

    def step(b, h, i, s):
        ag = ag_ref[b, :, s]
        sg = masked_scores(lower, ag, v_ref[b, :, s])
        scores = masked_scores(lower, q_ref[b, :, s], k_ref[b, :, s])
        earlier = pick_state(place, so, sr, b, h)
        dq_ref[b, :, s] = (dot(sg, k_ref[b, :, s], 1, 0) + SCALE * dot(ag, earlier, 1, 1)).astype(BF16)
        dk_ref[b, :, s] = dot(sg, q_ref[b, :, s], 0, 0)
        dv_ref[b, :, s] = dot(scores, ag, 0, 0)

    each_head(q_ref.shape[2], step)


def outer_body(place, k_ref, v_ref, ik_ref, iv_ref, go, gr, dk_ref, dv_ref):
    def step(b, h, i, s):
        later = pick_state(place, go, gr, b, h)
        dk_ref[b, :, s] = (ik_ref[b, :, s] + SCALE * dot(v_ref[b, :, s], later, 1, 1)).astype(BF16)
        dv_ref[b, :, s] = (iv_ref[b, :, s] + SCALE * dot(k_ref[b, :, s], later, 1, 0)).astype(BF16)

    each_batch(k_ref.shape[2], step)


def shift(value, axis, step):
    n = lax.axis_size(axis)
    return lax.ppermute(value, axis, [(i, (i + step) % n) for i in range(n)])


def shift_by_core(value, first, step):
    def target(x, y, c):
        along_y = (c == 0) == first
        return (x, (y + step) % 4, c) if along_y else ((x + step) % 4, y, c)

    def index(x, y, c):
        return (x * 4 + y) * 2 + c

    places = [(x, y, c) for x in range(4) for y in range(4) for c in range(2)]
    return lax.ppermute(value, CTX, [(index(*p), index(*target(*p))) for p in places])


def exclusive(place, keep, send, reverse):
    half, size = keep.shape, keep.size
    got = shift(send, "ctx_2", 1)
    chip = call(chip_body, [shape(half, BF16)], [keep, got], size)[0]
    near = []
    for d in (1, 2, 3):
        near.append(shift_by_core(chip, True, d))
    own, *out = call(
        functools.partial(first_axis_body, reverse),
        [shape(half, F32)] + [shape(half, BF16)] * 3,
        [place, chip, *near],
        size * 10,
        True,
    )
    far = []
    for d in (1, 2, 3):
        far.append(shift_by_core(out[d - 1], False, d))
    mine, other = call(
        functools.partial(second_axis_body, reverse),
        [shape(half, BF16)] * 2,
        [place, own, *far, keep, got],
        size * 8,
        True,
    )
    return mine, shift(other, "ctx_2", 1)


def gather_ring(block):
    near, right, left = [block], block, block
    rows, width = block.shape
    for i in (1, 2, 3, 4):
        if i == 4:
            half = [shape((rows, width // 2), BF16)]
            right = call(functools.partial(half_body, 0), half, [right], 0)[0]
            left = call(functools.partial(half_body, width // 2), half, [left], 0)[0]
        right = shift(right, "head", 1)
        left = shift(left, "head", -1)
        near += [right, left]
    return near


def output_ring(place, normed, weight):
    rows, width = normed.shape
    flops = 2 * rows * width * width
    half, whole = [shape((rows, width // 2), BF16)] * 2, [shape((rows, width), BF16)] * 2
    right, left = call(out_first_body, half, [place, normed, weight], flops, True)
    for step in (3, 2, 1):
        right = shift(right, "head", 1)
        left = shift(left, "head", -1)
        right, left = call(
            functools.partial(out_step_body, step),
            whole,
            [place, normed, weight, right, left],
            2 * flops,
            True,
        )
    right = shift(right, "head", 1)
    left = shift(left, "head", -1)
    return call(out_last_body, whole[:1], [place, normed, weight, right, left], flops, True)[0]


def send_weight(place, normed, blocks):
    rows, width = normed.shape
    theirs = call(
        functools.partial(weight_out_body, STEPS),
        [shape((4, 4, width, DH), BF16)],
        [place, normed, *blocks],
        rows * width * width * 8,
        True,
    )[0]
    return shift(theirs, "ctx_2", 1)


def reduce_weight(place, normed, blocks, theirs, factor):
    rows, width = normed.shape
    flops = rows * width * width
    whole = (4, width, DH)
    own, *send = call(
        functools.partial(weight_add_body, STEPS),
        [shape(whole, BF16)] * 4,
        [place, normed, *blocks, theirs],
        flops * 8,
        True,
        [VMEM((4, *whole), BF16), pltpu.SemaphoreType.DMA((4,))],
    )
    got = []
    for d in (1, 2, 3):
        got.append(shift_by_core(send[d - 1], True, d))
    piece = (width, DH)
    own, *send = call(
        combine_body,
        [shape(piece, F32)] + [shape(piece, BF16)] * 3,
        [place, own, *got],
        own.size * 4,
        True,
    )
    got = []
    for d in (1, 2, 3):
        got.append(shift_by_core(send[d - 1], False, d))
    return call(functools.partial(finish_body, factor), [shape(piece, F32)], [own, *got], own.size * 4)[0]


def layer(queries, key_rows, value_rows, out_weight, cotangent):
    _, length, width = queries.shape
    n_head = lax.axis_size("head")
    rows = 2 * length
    n_mat = 2 * width // DH
    half = (n_mat // 2, DH, DH)
    blocks = gather_ring(cotangent.reshape(rows, width))
    mx, my, mc, mz = (lax.axis_index(a) for a in (*CTX, "head"))
    place = jnp.stack([mx, my, mc, mz]).astype(jnp.int32)
    mat_flops = 2 * n_mat * length * DH * DH
    pair = [shape(half, F32), shape(half, BF16)]
    keep, send, near_keys, near_values, near_queries = call(
        state_body,
        pair + [shape(queries.shape, BF16)] * 3,
        [place, key_rows, value_rows, queries],
        mat_flops,
        True,
        [pltpu.SemaphoreType.DMA],
        pltpu.HBM,
    )
    intra = call(
        intra_body,
        [shape(queries.shape, F32)],
        [near_queries, near_keys, near_values],
        3 * mat_flops,
    )[0]
    state = exclusive(place, keep, send, False)
    normed, attended = call(
        forward_body,
        [shape(queries.shape, BF16), shape(queries.shape, F32)],
        [place, near_queries, intra, *state],
        mat_flops,
        True,
    )
    normed = normed.reshape(rows, width)
    big = 2 * rows * width * width * n_head
    layer_output = output_ring(place, normed, out_weight).reshape(queries.shape)
    theirs = send_weight(place, normed, blocks)
    part_grad = call(
        functools.partial(grad_near_body, STEPS),
        [shape((rows, width), F32)],
        [place, *blocks[:7], out_weight],
        big * 7 // 8,
        True,
    )[0]
    attended_grad, keep, send = call(
        grad_far_body,
        [shape(queries.shape, BF16), *pair],
        [place, *blocks[7:], out_weight, part_grad, attended, queries],
        big // 8,
        True,
        [VMEM(queries.shape, F32)],
    )
    factor = (rows * lax.axis_size(CTX)) ** (-0.5)
    weight_grad = reduce_weight(place, normed, blocks, theirs, factor)
    grad_state = exclusive(place, keep, send, True)
    query_grad, inner_key, inner_value = call(
        inner_body,
        [shape(queries.shape, BF16)] + [shape(queries.shape, F32)] * 2,
        [place, queries, key_rows, value_rows, attended_grad, *state],
        5 * mat_flops,
        True,
    )
    key_grad, value_grad = call(
        outer_body,
        [shape(queries.shape, BF16)] * 2,
        [place, key_rows, value_rows, inner_key, inner_value, *grad_state],
        2 * mat_flops,
        True,
    )
    return (layer_output, query_grad, key_grad, value_grad, weight_grad)


def solution(mesh):
    split = Mesh(
        mesh.devices.reshape(4, 4, 2, mesh.shape["head"]), ("ctx_0", "ctx_1", "ctx_2", "head")
    )
    rows = P(None, CTX, "head")
    return jax.shard_map(
        layer,
        mesh=split,
        in_specs=(rows, rows, rows, P("head", None), rows),
        out_specs=(rows, rows, rows, rows, P("head", CTX)),
        check_vma=False,
    )
```
